768 devices in a mesh: band: 192 (over z, x_hi, y), group: 4 (over x_lo, core).
Axes of the slice: x: 4 (x_hi: 2, x_lo: 2; x = x_hi * 2 + x_lo), y: 8, z: 12, core: 2. Of those that a mesh axis runs over, the one named last changes fastest.
Arguments:
- trial: bfloat16 [192, 64, 4096], P('band'), may hold values from -6 to 6
- orbitals: bfloat16 [768, 64, 4096], P(('band', 'group')), may hold values from -6 to 6
- labels: int32 [768], P(('band', 'group')), may hold values from 0 to 767, each once
- kernel_mask: int32 [64, 4096], replicated, may hold values from 0 to 1, as said below
Outputs:
- exchange_field: float32 [192, 64, 4096], P('band', 'group')
The draws below stay inside these ranges and needn't reach their ends.
Inputs may be any that keep to these rules, and one draw needn't show every extreme that they name: `labels`: a permutation of the source orbitals' numbers. `kernel_mask`: unchanged when any one frequency index k is replaced by (64 - k) mod 64.
All inputs are finite; a program needn't handle non-finite values.
Results may differ from the reference program's by a relative error of at most 0.009.
Values may be sent and summed in bfloat16 or wider, within the bound.
No kernel may reach another device: no remote copies, remote signals or barrier semaphores. Data moves between devices by JAX's collectives and lax.ppermute only.
A program may use at most 32 MiB of HBM per device.

```python
import jax
import jax.numpy as jnp
from jax import lax

GRID = 64
WINDOW = 2
NORB = 768
N_BAND = 192
N_GROUP = 4


def draw_kernel_mask(key, part):
    half_size = GRID // 2 + 1
    random_bits = jax.random.randint(key, (half_size, half_size, half_size), 0, 4)
    kept_mask = jnp.where(random_bits > 0, 1, 0).astype(jnp.int32)
    frequency = jnp.arange(GRID, dtype=jnp.int32)
    folded = jnp.minimum(frequency, GRID - frequency)
    cube = kept_mask[folded][:, folded][:, :, folded]
    return cube.reshape(GRID, GRID * GRID)


def level_of(rng, shape, cuts, smallest, top_value):
    factor_of = 1.0
    for dim, shards_of in cuts:
        steps = jax.random.uniform(jax.random.fold_in(jax.random.fold_in(rng, 6), dim), (shards_of,), jnp.float32, smallest / len(cuts), top_value / len(cuts))
        factor_of = factor_of * jnp.repeat(jnp.exp(steps), shape[dim] // shards_of).reshape((-1,) + (1,) * (len(shape) - 1 - dim))
    return factor_of


def noise(rng, dims, deviation, limit, pieces=(), held_as=jnp.bfloat16):
    drawn = deviation * jax.random.normal(rng, dims, jnp.float32)
    if pieces:
        drawn = drawn * level_of(rng, dims, pieces, -0.22, 0.18)
    return jnp.clip(drawn, -limit, limit).astype(held_as)


def setup_inputs(seed: int = 0) -> dict:
    key_list = jax.random.split(jax.random.key(seed), 5)
    trial = noise(key_list[0], (N_BAND, GRID, GRID * GRID), 1.0, 6.0, ((0, 192),))
    orbitals = noise(key_list[1], (NORB, GRID, GRID * GRID), 1.0, 6.0, ((0, 768),))
    labels = jax.random.permutation(key_list[2], NORB).astype(jnp.int32)
    kernel_mask = draw_kernel_mask(jax.random.fold_in(key_list[4], 71), 0)
    return {"trial": trial, "orbitals": orbitals, "labels": labels, "kernel_mask": kernel_mask}


screen_square = 16.0

def cas_table(grid_size):
    frequency = jnp.arange(grid_size, dtype=jnp.int32)
    product = frequency[:, None] * frequency[None, :] % grid_size
    phase_angle = product.astype(jnp.float32) * (2.0 * jnp.pi / grid_size)
    return ((jnp.cos(phase_angle) + jnp.sin(phase_angle)) / jnp.sqrt(jnp.float32(grid_size))).astype(jnp.bfloat16)

def screened_kernel(mask_cube):
    grid_size = mask_cube.shape[0]
    frequency = jnp.arange(grid_size, dtype=jnp.int32)
    signed = jnp.where(frequency < grid_size // 2, frequency, frequency - grid_size)
    squared = signed * signed
    q_square = squared[:, None, None] + squared[None, :, None] + squared[None, None, :]
    return mask_cube.astype(jnp.float32) * screen_square / (q_square.astype(jnp.float32) + screen_square)

def occupation(label_values, orbital_count):
    shifted = (label_values.astype(jnp.float32) - orbital_count / 2.0) / (orbital_count / 4.0)
    return 1.0 / (1.0 + jnp.exp(shifted))

def axis_pass(field_data, hartley):
    return jnp.einsum('pxyz,xk->pyzk', field_data.astype(jnp.float32), hartley.astype(jnp.float32), precision=lax.Precision.HIGHEST)

def reference(trial, orbitals, labels, kernel_mask):
    grid_size = GRID
    band_count = N_BAND
    group_count = N_GROUP
    hartley = cas_table(grid_size)
    kernel = screened_kernel(kernel_mask.reshape(grid_size, grid_size, grid_size))
    weights = occupation(labels, band_count * group_count).reshape(band_count, group_count)
    source_cube = orbitals.reshape(band_count, group_count, grid_size, grid_size, grid_size)
    target_cube = trial.reshape(band_count, grid_size, grid_size, grid_size)

    def one_target(band_index):
        positions = (band_index + jnp.arange(WINDOW, dtype=jnp.int32)) % band_count
        sources = jnp.take(source_cube, positions, axis=0).reshape(WINDOW * group_count, grid_size, grid_size, grid_size)
        source_weights = jnp.take(weights, positions, axis=0).reshape(-1)
        target = lax.dynamic_index_in_dim(target_cube, band_index, 0, keepdims=False)
        density = (target.astype(jnp.float32)[None] * sources.astype(jnp.float32)).astype(jnp.bfloat16)
        first = axis_pass(density, hartley).astype(jnp.bfloat16)
        second = axis_pass(first, hartley).astype(jnp.bfloat16)
        spectrum = (axis_pass(second, hartley) * kernel[None]).astype(jnp.bfloat16)
        back_first = axis_pass(spectrum, hartley).astype(jnp.bfloat16)
        back_second = axis_pass(back_first, hartley).astype(jnp.bfloat16)
        potential = axis_pass(back_second, hartley)
        contribution = source_weights[:, None, None, None] * potential * sources.astype(jnp.float32)
        return -lax.optimization_barrier(jnp.sum(contribution, axis=0)).reshape(grid_size, grid_size * grid_size)
    return lax.map(one_target, jnp.arange(band_count, dtype=jnp.int32))
```

```python
import functools

import jax
import jax.numpy as jnp
import numpy as np
from jax import lax
from jax.experimental import pallas as pl
from jax.experimental.pallas import tpu as pltpu
from jax.sharding import PartitionSpec as P

WINDOW = 2
SCREEN_SQUARE = 16.0
N = 64
HALF = 32
LANES = 128
WIDE = 256
BLOCKS = N * N // WIDE


def cas_table():
    k = np.arange(N)
    angle = (k[:, None] * k[None, :] % N).astype(np.float64) * (2.0 * np.pi / N)
    return (np.cos(angle) + np.sin(angle)) / np.sqrt(float(N))


def tables():
    h = cas_table()
    order = np.concatenate([np.arange(0, N, 2), np.arange(1, N, 2)])
    diagonal = np.kron(np.eye(WIDE // N), h)
    return tuple(jnp.asarray(m, jnp.bfloat16) for m in (h, h[order], h[:, order], diagonal, np.eye(N)[order]))


def dot(a, b):
    return jnp.dot(a, b, preferred_element_type=jnp.float32)


def low_lanes():
    return lax.broadcasted_iota(jnp.int32, (HALF, LANES), 1) < N


def exchange(top, bottom, low):
    return (
        jnp.where(low, top, pltpu.roll(bottom, N, 1)),
        jnp.where(low, pltpu.roll(top, N, 1), bottom),
    )


def scatter_rows(block, column, turned, low):
    first, second = exchange(block[:HALF], block[HALF:], low)
    turned[pl.ds(2 * column, HALF, stride=N), :] = first
    turned[pl.ds(2 * column + 1, HALF, stride=N), :] = second


def gather_rows(column, turned, low):
    first = turned[pl.ds(2 * column, HALF, stride=N), :]
    second = turned[pl.ds(2 * column + 1, HALF, stride=N), :]
    top, bottom = exchange(first, second, low)
    return jnp.concatenate([top, bottom], axis=0)


def pair_field(target, source, scale, kernel, h, h_rows, h_cols, h_diag, turned, emit):
    low = low_lanes()
    for block in range(BLOCKS):
        columns = slice(block * WIDE, (block + 1) * WIDE)
        density = (
            target[:, columns].astype(jnp.float32) * source[:, columns].astype(jnp.float32)
        ).astype(jnp.bfloat16)
        first = dot(h_rows[...], density)
        for part in range(2):
            scatter_rows(first[:, part * LANES : (part + 1) * LANES], 2 * block + part, turned, low)
    for block in range(BLOCKS):
        rows = [slice((2 * block + part) * N, (2 * block + part + 1) * N) for part in range(2)]
        first = jnp.concatenate([turned[r, :].astype(jnp.bfloat16) for r in rows], axis=1)
        second = dot(h[...], first).astype(jnp.bfloat16)
        spectrum = dot(second, h_diag[...]) * kernel[:, block * WIDE : (block + 1) * WIDE]
        back = dot(spectrum.astype(jnp.bfloat16), h_diag[...]).astype(jnp.bfloat16)
        back = dot(h[...], back)
        for part in range(2):
            turned[rows[part], :] = back[:, part * LANES : (part + 1) * LANES]
    for block in range(BLOCKS):
        columns = slice(block * WIDE, (block + 1) * WIDE)
        back = jnp.concatenate(
            [gather_rows(2 * block + part, turned, low) for part in range(2)], axis=1
        ).astype(jnp.bfloat16)
        potential = dot(h_cols[...], back)
        emit(columns, potential * scale * source[:, columns].astype(jnp.float32))


def minus_occupation(label, count):
    shifted = (jnp.full((1, WIDE), label, jnp.int32).astype(jnp.float32) - count / 2.0) / (count / 4.0)
    return -1.0 / (1.0 + jnp.exp(shifted))


def own_kernel(count, label, target, source, mask, h, h_rows, h_cols, h_diag, rows, field, kernel, turned):
    low = low_lanes()
    for block in range(BLOCKS):
        kept = mask[:, block * WIDE : (block + 1) * WIDE].astype(jnp.float32).astype(jnp.bfloat16)
        kept = dot(rows[...], kept)
        for part in range(2):
            scatter_rows(kept[:, part * LANES : (part + 1) * LANES], 2 * block + part, turned, low)
    ky = lax.broadcasted_iota(jnp.int32, (N, LANES), 0)
    lane = lax.broadcasted_iota(jnp.int32, (N, LANES), 1)

    def squared(k):
        signed = jnp.where(k < N // 2, k, k - N)
        return signed * signed

    plane = squared(ky) + squared(lane % N)
    for half in range(HALF):
        q_square = plane + squared(2 * half + lane // N)
        kept = turned[half * N : (half + 1) * N, :]
        kernel[:, half * LANES : (half + 1) * LANES] = (
            kept * SCREEN_SQUARE / (q_square.astype(jnp.float32) + SCREEN_SQUARE)
        )

    def emit(columns, value):
        field[:, columns] = value

    pair_field(target, source, minus_occupation(label[0], count), kernel, h, h_rows, h_cols, h_diag, turned, emit)


def cross_kernel(count, label, target, source, field, kernel, h, h_rows, h_cols, h_diag, total, turned):
    def emit(columns, value):
        total[:, columns] = (field[:, columns] + value).astype(jnp.bfloat16)

    pair_field(target, source, minus_occupation(label[0], count), kernel, h, h_rows, h_cols, h_diag, turned, emit)


def call(kernel, outs, flops, name, *args):
    vmem = pl.BlockSpec(memory_space=pltpu.VMEM)
    return pl.pallas_call(
        kernel,
        out_shape=outs,
        in_specs=[pl.BlockSpec(memory_space=pltpu.SMEM)] + [vmem] * (len(args) - 1),
        out_specs=jax.tree.map(lambda _: vmem, outs),
        scratch_shapes=[pltpu.VMEM((HALF * N, LANES), jnp.float32)],
        compiler_params=pltpu.CompilerParams(vmem_limit_bytes=24 * 1024 * 1024),
        cost_estimate=pl.CostEstimate(flops=flops, bytes_accessed=4 * 1024 * 1024, transcendentals=0),
        name=name,
    )(*args)


def passed_along(value, axis, steps):
    count = lax.axis_size(axis)
    return lax.ppermute(value, axis, [(s, (s + steps) % count) for s in range(count)])


def shards(trial, orbitals, labels, kernel_mask):
    count = lax.axis_size("band") * lax.axis_size("group")
    members = lax.axis_size("group")
    *h, rows = tables()
    target, source = trial[0], orbitals[0]
    next_source = passed_along(source, "band", -1)
    next_label = passed_along(labels, "band", -1)
    plane = jax.ShapeDtypeStruct((N, N * N), jnp.float32)
    flops = 6 * 2 * N**4
    field, kernel = call(
        functools.partial(own_kernel, count), (plane, plane), flops, "own", labels, target, source, kernel_mask, *h, rows
    )
    total = call(
        functools.partial(cross_kernel, count),
        jax.ShapeDtypeStruct((N, N * N), jnp.bfloat16),
        flops,
        "cross",
        next_label, target, next_source, field, kernel, *h,
    )
    slabs = total.reshape(members, N // members, N * N)
    pieces = lax.all_to_all(slabs, "group", 0, 0)
    return jnp.sum(pieces.astype(jnp.float32), axis=0, keepdims=True)


def solution(mesh):
    in_specs = (P("band", None, None), P(("band", "group"), None, None), P(("band", "group")), P())
    out_specs = P("band", "group", None)
    return jax.shard_map(shards, mesh=mesh, in_specs=in_specs, out_specs=out_specs, check_vma=False)
```

```python
import functools

import jax
import jax.numpy as jnp
import numpy as np
from jax import lax
from jax.experimental import pallas as pl
from jax.experimental.pallas import tpu as pltpu
from jax.sharding import PartitionSpec as P

SCREEN_SQUARE = 16.0
N = 64
HALF = 32
LANES = 128
WIDE = 256
BLOCKS = N * N // WIDE
STRIDE = 65
CHUNK = 256
MEMBERS = 4
SLAB = N // MEMBERS

DIAG, CAS, CAS_ROWS, CAS_COLS, EVEN_FIRST, TABLE_ROWS = 0, 256, 320, 384, 448, 512


def tables():
    k = np.arange(N)
    angle = (k[:, None] * k[None, :] % N).astype(np.float64) * (2.0 * np.pi / N)
    h = (np.cos(angle) + np.sin(angle)) / np.sqrt(float(N))
    order = np.concatenate([np.arange(0, N, 2), np.arange(1, N, 2)])
    table = np.zeros((TABLE_ROWS, WIDE))
    table[DIAG:CAS] = np.kron(np.eye(WIDE // N), h)
    table[CAS:CAS_ROWS, :N] = h
    table[CAS_ROWS:CAS_COLS, :N] = h[order]
    table[CAS_COLS:EVEN_FIRST, :N] = h[:, order]
    table[EVEN_FIRST:, :N] = np.eye(N)[order]
    return jnp.asarray(table, jnp.bfloat16)


def dot(a, b):
    return jnp.dot(a, b, preferred_element_type=jnp.float32)


def low_lanes():
    return lax.broadcasted_iota(jnp.int32, (HALF, LANES), 1) < N


def exchange(top, bottom, low):
    return (
        jnp.where(low, top, pltpu.roll(bottom, N, 1)),
        jnp.where(low, pltpu.roll(top, N, 1), bottom),
    )


def scatter_rows(block, column, turned, low):
    first, second = exchange(block[:HALF], block[HALF:], low)
    turned[pl.ds(2 * column, HALF, stride=STRIDE), :] = first
    turned[pl.ds(2 * column + 1, HALF, stride=STRIDE), :] = second


def gather_rows(column, turned, low):
    first = turned[pl.ds(2 * column, HALF, stride=STRIDE), :]
    second = turned[pl.ds(2 * column + 1, HALF, stride=STRIDE), :]
    top, bottom = exchange(first, second, low)
    return jnp.concatenate([top, bottom], axis=0)


def turned_block(block, turned):
    return jnp.concatenate(
        [turned[pl.ds((2 * block + part) * STRIDE, N), :].astype(jnp.bfloat16) for part in range(2)], axis=1
    )


def columns_of(block):
    return slice(block * WIDE, (block + 1) * WIDE)


def by_owner(me, ref, columns):
    return jnp.concatenate([ref[pl.ds((me ^ k) * SLAB, SLAB), columns] for k in range(MEMBERS)], axis=0)


def pair_field(me, target, source, scale, kernel_ready, table, turned, rows, emit):
    low = low_lanes()
    h_diag, h, h_rows = table[DIAG:CAS, :], table[CAS:CAS_ROWS, :N], table[CAS_ROWS:CAS_COLS, :N]
    for block in range(BLOCKS):
        first = dot(h_rows, target[:, columns_of(block)] * source[:, columns_of(block)])
        for part in range(2):
            scatter_rows(first[:, part * LANES : (part + 1) * LANES], 2 * block + part, turned, low)
    for block in range(BLOCKS):
        rows[block * N : (block + 1) * N, :] = dot(h, turned_block(block, turned)).astype(jnp.bfloat16)
    kernel = kernel_ready()
    for chunk in range(BLOCKS * N // CHUNK):
        part = slice(chunk * CHUNK, (chunk + 1) * CHUNK)
        spectrum = dot(rows[part, :], h_diag) * kernel[part, :]
        rows[part, :] = dot(spectrum.astype(jnp.bfloat16), h_diag).astype(jnp.bfloat16)
    for block in range(BLOCKS):
        back = dot(h, rows[block * N : (block + 1) * N, :])
        for part in range(2):
            turned[pl.ds((2 * block + part) * STRIDE, N), :] = back[:, part * LANES : (part + 1) * LANES]
    h_cols = by_owner(me, table.at[CAS_COLS:EVEN_FIRST], slice(0, N))
    for block in range(BLOCKS):
        back = jnp.concatenate(
            [gather_rows(2 * block + part, turned, low) for part in range(2)], axis=1
        ).astype(jnp.bfloat16)
        potential = dot(h_cols, back)
        emit(block, potential * scale * by_owner(me, source, columns_of(block)).astype(jnp.float32))


def own_kernel(count, label, target, source, mask, table, field, kernel, weight, target_out, table_out,
               source_in, mask_in, turned, rows, sems):
    copies = [
        pltpu.make_async_copy(a, b, sems.at[i])
        for i, (a, b) in enumerate(
            ((target, target_out), (source, source_in), (table, table_out), (mask, mask_in))
        )
    ]
    for copy in copies:
        copy.start()
    me = lax.axis_index("group")
    shifted = (jnp.full((8, LANES), label[0], jnp.int32).astype(jnp.float32) - count / 2.0) / (count / 4.0)
    scale = -1.0 / (1.0 + jnp.exp(shifted))
    weight[...] = scale
    low = low_lanes()
    ky = lax.broadcasted_iota(jnp.int32, (N, LANES), 0)
    lane = lax.broadcasted_iota(jnp.int32, (N, LANES), 1)

    def squared(k):
        signed = jnp.where(k < N // 2, k, k - N)
        return signed * signed

    plane = squared(ky) + squared(lane % N)

    for copy in copies:
        copy.wait()
    even_first = table_out[EVEN_FIRST:, :N]
    for block in range(BLOCKS):
        kept = dot(even_first, mask_in[:, columns_of(block)].astype(jnp.float32).astype(jnp.bfloat16))
        for part in range(2):
            scatter_rows(kept[:, part * LANES : (part + 1) * LANES], 2 * block + part, turned, low)
    for half in range(HALF):
        q_square = plane + squared(2 * half + lane // N)
        kept = turned[pl.ds(half * STRIDE, N), :]
        block, part = half // 2, half % 2
        kernel[block * N : (block + 1) * N, part * LANES : (part + 1) * LANES] = (
            kept * SCREEN_SQUARE / (q_square.astype(jnp.float32) + SCREEN_SQUARE)
        )

    def emit(block, value):
        field[:, columns_of(block)] = value

    pair_field(me, target_out, source_in, scale[:1, :1], lambda: kernel, table_out, turned, rows, emit)


def cross_kernel(weight, target, source, field, kernel, table, mine, *rest):
    sent, (turned, rows) = rest[: MEMBERS - 1], rest[MEMBERS - 1 :]

    def emit(block, value):
        total = field[:, columns_of(block)] + value
        mine[:, columns_of(block)] = total[:SLAB]
        for k in range(1, MEMBERS):
            sent[k - 1][:, columns_of(block)] = total[k * SLAB : (k + 1) * SLAB].astype(jnp.bfloat16)

    pair_field(
        lax.axis_index("group"), target, source, weight[:1, :1], lambda: kernel, table, turned, rows, emit
    )


def shape(rows, columns, dtype):
    return jax.ShapeDtypeStruct((rows, columns), dtype)


PAIR_SCRATCH = [pltpu.VMEM((HALF * STRIDE, LANES), jnp.float32), pltpu.VMEM((BLOCKS * N, WIDE), jnp.bfloat16)]
VMEM = pl.BlockSpec(memory_space=pltpu.VMEM)
HBM = pl.BlockSpec(memory_space=pltpu.HBM)


def call(kernel, outs, in_specs, scratch, name):
    return pl.pallas_call(
        kernel,
        out_shape=outs,
        in_specs=in_specs,
        out_specs=[VMEM] * len(outs),
        scratch_shapes=scratch,
        compiler_params=pltpu.CompilerParams(vmem_limit_bytes=40 * 1024 * 1024),
        cost_estimate=pl.CostEstimate(flops=6 * 2 * N**4, bytes_accessed=4 * 1024 * 1024, transcendentals=0),
        name=name,
    )


def passed_along(value, axis, steps):
    count = lax.axis_size(axis)
    return lax.ppermute(value, axis, [(s, (s + steps) % count) for s in range(count)])


def swapped(value, bits):
    return lax.ppermute(value, "group", [(s, s ^ bits) for s in range(MEMBERS)])


def shards(trial, orbitals, labels, kernel_mask):
    count = lax.axis_size("band") * lax.axis_size("group")
    target, source = trial[0], orbitals[0]
    next_source = passed_along(source, "band", -1)
    field, kernel, weight, target, table = call(
        functools.partial(own_kernel, count),
        (
            shape(N, N * N, jnp.float32),
            shape(BLOCKS * N, WIDE, jnp.float32),
            shape(8, LANES, jnp.float32),
            shape(N, N * N, jnp.bfloat16),
            shape(TABLE_ROWS, WIDE, jnp.bfloat16),
        ),
        [pl.BlockSpec(memory_space=pltpu.SMEM)] + [HBM] * 4,
        [pltpu.VMEM((N, N * N), jnp.bfloat16), pltpu.VMEM((N, N * N), jnp.int32)]
        + PAIR_SCRATCH
        + [pltpu.SemaphoreType.DMA((4,))],
        "own",
    )(labels, target, source, kernel_mask, tables())
    next_weight = passed_along(weight, "band", -1)
    mine, *sent = call(
        cross_kernel,
        [shape(SLAB, N * N, jnp.float32)] + [shape(SLAB, N * N, jnp.bfloat16)] * (MEMBERS - 1),
        [VMEM] * 6,
        PAIR_SCRATCH,
        "cross",
    )(next_weight, target, next_source, field, kernel, table)
    received = {bits: swapped(sent[bits - 1], bits) for bits in (2, 3, 1)}
    for bits in (2, 3, 1):
        mine = mine + received[bits].astype(jnp.float32)
    return mine[None]


def solution(mesh):
    in_specs = (P("band", None, None), P(("band", "group"), None, None), P(("band", "group")), P())
    out_specs = P("band", "group", None)
    return jax.shard_map(shards, mesh=mesh, in_specs=in_specs, out_specs=out_specs, check_vma=False)
```

```python
import functools

import jax
import jax.numpy as jnp
import numpy as np
from jax import lax
from jax.experimental import pallas as pl
from jax.experimental.pallas import tpu as pltpu
from jax.sharding import PartitionSpec as P

SCREEN_SQUARE = 16.0
N = 64
HALF = 32
LANES = 128
WIDE = 256
BLOCKS = N * N // WIDE
STRIDE = 65
CHUNK = 256
MEMBERS = 4
SLAB = N // MEMBERS
PACKED = N * N + LANES

DIAG, CAS, CAS_ROWS, CAS_COLS, EVEN_FIRST, TABLE_ROWS = 0, 256, 320, 384, 448, 512


def tables():
    k = np.arange(N)
    angle = (k[:, None] * k[None, :] % N).astype(np.float64) * (2.0 * np.pi / N)
    h = (np.cos(angle) + np.sin(angle)) / np.sqrt(float(N))
    order = np.concatenate([np.arange(0, N, 2), np.arange(1, N, 2)])
    table = np.zeros((TABLE_ROWS, WIDE))
    table[DIAG:CAS] = np.kron(np.eye(WIDE // N), h)
    table[CAS:CAS_ROWS, :N] = h
    table[CAS_ROWS:CAS_COLS, :N] = h[order]
    table[CAS_COLS:EVEN_FIRST, :N] = h[:, order]
    table[EVEN_FIRST:, :N] = np.eye(N)[order]
    return jnp.asarray(table, jnp.bfloat16)


def dot(a, b):
    return jnp.dot(a, b, preferred_element_type=jnp.float32)


def low_lanes():
    return lax.broadcasted_iota(jnp.int32, (HALF, LANES), 1) < N


def exchange(top, bottom, low):
    return (
        jnp.where(low, top, pltpu.roll(bottom, N, 1)),
        jnp.where(low, pltpu.roll(top, N, 1), bottom),
    )


def scatter_rows(block, column, turned, low):
    first, second = exchange(block[:HALF], block[HALF:], low)
    turned[pl.ds(2 * column, HALF, stride=STRIDE), :] = first
    turned[pl.ds(2 * column + 1, HALF, stride=STRIDE), :] = second


def gather_rows(column, turned, low):
    first = turned[pl.ds(2 * column, HALF, stride=STRIDE), :]
    second = turned[pl.ds(2 * column + 1, HALF, stride=STRIDE), :]
    top, bottom = exchange(first, second, low)
    return jnp.concatenate([top, bottom], axis=0)


def turned_block(block, turned):
    return jnp.concatenate(
        [turned[pl.ds((2 * block + part) * STRIDE, N), :].astype(jnp.bfloat16) for part in range(2)], axis=1
    )


def columns_of(block):
    return slice(block * WIDE, (block + 1) * WIDE)


def by_owner(me, ref, columns):
    return jnp.concatenate([ref[pl.ds((me ^ k) * SLAB, SLAB), columns] for k in range(MEMBERS)], axis=0)


def pair_field(me, target, source, scale, kernel_ready, table, turned, rows, emit):
    low = low_lanes()
    h_diag, h, h_rows = table[DIAG:CAS, :], table[CAS:CAS_ROWS, :N], table[CAS_ROWS:CAS_COLS, :N]
    for block in range(BLOCKS):
        first = dot(h_rows, target[:, columns_of(block)] * source[:, columns_of(block)])
        for part in range(2):
            scatter_rows(first[:, part * LANES : (part + 1) * LANES], 2 * block + part, turned, low)
    for block in range(BLOCKS):
        rows[block * N : (block + 1) * N, :] = dot(h, turned_block(block, turned)).astype(jnp.bfloat16)
    kernel = kernel_ready()
    for chunk in range(BLOCKS * N // CHUNK):
        part = slice(chunk * CHUNK, (chunk + 1) * CHUNK)
        spectrum = dot(rows[part, :], h_diag) * kernel[part, :]
        rows[part, :] = dot(spectrum.astype(jnp.bfloat16), h_diag).astype(jnp.bfloat16)
    for block in range(BLOCKS):
        back = dot(h, rows[block * N : (block + 1) * N, :])
        for part in range(2):
            turned[pl.ds((2 * block + part) * STRIDE, N), :] = back[:, part * LANES : (part + 1) * LANES]
    h_cols = by_owner(me, table.at[CAS_COLS:EVEN_FIRST], slice(0, N))
    for block in range(BLOCKS):
        back = jnp.concatenate(
            [gather_rows(2 * block + part, turned, low) for part in range(2)], axis=1
        ).astype(jnp.bfloat16)
        potential = dot(h_cols, back)
        emit(block, potential * scale * by_owner(me, source, columns_of(block)).astype(jnp.float32))


def on_last_band():
    return lax.axis_index("band") == lax.axis_size("band") - 1


def pack_kernel(label, source, packed, sem):
    copy = pltpu.make_async_copy(source, packed.at[:, : N * N], sem)
    copy.start()
    for half, part in enumerate((label[0] // 8, label[0] % 8)):
        packed[half * HALF : (half + 1) * HALF, N * N :] = (
            jnp.full((HALF, LANES), part, jnp.int32).astype(jnp.float32).astype(jnp.bfloat16)
        )
    copy.wait()


def minus_occupation(count, packed):
    high, low = (packed[half * HALF : half * HALF + 16, N * N :].astype(jnp.float32) for half in range(2))
    shifted = (8.0 * high + low - count / 2.0) / (count / 4.0)
    return (-1.0 / (1.0 + jnp.exp(shifted)))[:1, :1]


def own_body(count, target, packed, mask, table, field, kernel, target_in, table_in, mask_in, turned, rows, sems):
    copies = [
        pltpu.make_async_copy(a, b, sems.at[i])
        for i, (a, b) in enumerate(((target, target_in), (table, table_in), (mask, mask_in)))
    ]
    for copy in copies:
        copy.start()
    me = lax.axis_index("group")
    low = low_lanes()
    ky = lax.broadcasted_iota(jnp.int32, (N, LANES), 0)
    lane = lax.broadcasted_iota(jnp.int32, (N, LANES), 1)

    def squared(k):
        signed = jnp.where(k < N // 2, k, k - N)
        return signed * signed

    plane = squared(ky) + squared(lane % N)
    for copy in copies:
        copy.wait()
    even_first = table_in[EVEN_FIRST:, :N]
    for block in range(BLOCKS):
        kept = dot(even_first, mask_in[:, columns_of(block)].astype(jnp.float32).astype(jnp.bfloat16))
        for part in range(2):
            scatter_rows(kept[:, part * LANES : (part + 1) * LANES], 2 * block + part, turned, low)
    for half in range(HALF):
        q_square = plane + squared(2 * half + lane // N)
        kept = turned[pl.ds(half * STRIDE, N), :]
        block, part = half // 2, half % 2
        kernel[block * N : (block + 1) * N, part * LANES : (part + 1) * LANES] = (
            kept * SCREEN_SQUARE / (q_square.astype(jnp.float32) + SCREEN_SQUARE)
        )

    def emit(block, value):
        field[:, columns_of(block)] = value

    pair_field(me, target_in, packed, minus_occupation(count, packed), lambda: kernel, table_in, turned, rows, emit)


def own_kernel(count, *refs):
    @pl.when(jnp.logical_not(on_last_band()))
    def _():
        own_body(count, *refs)


def own_last_kernel(count, *refs):
    @pl.when(on_last_band())
    def _():
        own_body(count, *refs)


def cross_body(count, target, packed, field, kernel, table, mine, sent, scratch):
    def emit(block, value):
        total = field[:, columns_of(block)] + value
        mine[:, columns_of(block)] = total[:SLAB]
        for k in range(1, MEMBERS):
            sent[k - 1][:, columns_of(block)] = total[k * SLAB : (k + 1) * SLAB].astype(jnp.bfloat16)

    pair_field(
        lax.axis_index("group"), target, packed, minus_occupation(count, packed), lambda: kernel, table, *scratch, emit
    )


def cross_kernel(count, target, packed, field, kernel, table, mine, *rest):
    @pl.when(jnp.logical_not(on_last_band()))
    def _():
        cross_body(count, target, packed, field, kernel, table, mine, rest[: MEMBERS - 1], rest[MEMBERS - 1 :])


def cross_last_kernel(count, target, packed, field, kernel, table, held, mine, *rest):
    @pl.when(on_last_band())
    def _():
        cross_body(count, target, packed, field, kernel, table, mine, rest[: MEMBERS - 1], rest[MEMBERS - 1 :])

    @pl.when(jnp.logical_not(on_last_band()))
    def _():
        mine[...] = held[...]


def shape(rows, columns, dtype):
    return jax.ShapeDtypeStruct((rows, columns), dtype)


PAIR_SCRATCH = [pltpu.VMEM((HALF * STRIDE, LANES), jnp.float32), pltpu.VMEM((BLOCKS * N, WIDE), jnp.bfloat16)]
OWN_SCRATCH = [pltpu.VMEM((N, N * N), jnp.int32)] + PAIR_SCRATCH + [pltpu.SemaphoreType.DMA((3,))]
VMEM = pl.BlockSpec(memory_space=pltpu.VMEM)
HBM = pl.BlockSpec(memory_space=pltpu.HBM)


def call(kernel, outs, in_specs, scratch, name, aliases=None, flops=6 * 2 * N**4):
    return pl.pallas_call(
        kernel,
        out_shape=outs,
        in_specs=in_specs,
        out_specs=[VMEM] * len(outs),
        scratch_shapes=scratch,
        input_output_aliases=aliases or {},
        compiler_params=pltpu.CompilerParams(vmem_limit_bytes=40 * 1024 * 1024),
        cost_estimate=pl.CostEstimate(flops=flops, bytes_accessed=4 * 1024 * 1024, transcendentals=0),
        name=name,
    )


def in_hbm(value):
    return pltpu.with_memory_space_constraint(value, pltpu.HBM)


def sent_along(value, pairs):
    return lax.ppermute(value, ("band", "group"), [(s[0] * MEMBERS + s[1], t[0] * MEMBERS + t[1]) for s, t in pairs])


def exchanged(sent, bands):
    return [
        sent_along(sent[bits - 1], [((b, g), (b, g ^ bits)) for b in bands for g in range(MEMBERS)]) for bits in (2, 3, 1)
    ]


def shards(trial, orbitals, labels, kernel_mask):
    bands = lax.axis_size("band")
    count = bands * MEMBERS
    last = bands - 1
    members = range(MEMBERS)
    target, table, mask = in_hbm(trial[0]), in_hbm(tables()), in_hbm(kernel_mask)
    packed = call(
        pack_kernel,
        [shape(N, PACKED, jnp.bfloat16)],
        [pl.BlockSpec(memory_space=pltpu.SMEM), HBM],
        [pltpu.SemaphoreType.DMA],
        "pack",
        flops=0,
    )(labels, in_hbm(orbitals[0]))[0]
    following = sent_along(packed, [((b, g), (b - 1, g)) for b in range(1, bands) for g in members])
    planes = [
        shape(N, N * N, jnp.float32),
        shape(BLOCKS * N, WIDE, jnp.float32),
        shape(N, N * N, jnp.bfloat16),
        shape(TABLE_ROWS, WIDE, jnp.bfloat16),
    ]
    sources = [HBM, VMEM, HBM, HBM]
    field, kernel, kept_target, kept_table = call(
        functools.partial(own_kernel, count), planes, sources, OWN_SCRATCH, "own"
    )(target, packed, mask, table)
    packed, field = lax.optimization_barrier((packed, field))
    wrapped = sent_along(packed, [((0, g), (last, g)) for g in members])
    last_field, last_kernel, last_target, last_table = call(
        functools.partial(own_last_kernel, count), planes, sources, OWN_SCRATCH, "own_last"
    )(target, packed, mask, table)
    slabs = [shape(SLAB, N * N, jnp.float32)] + [shape(SLAB, N * N, jnp.bfloat16)] * (MEMBERS - 1)
    mine, *sent = call(functools.partial(cross_kernel, count), slabs, [VMEM] * 5, PAIR_SCRATCH, "cross")(
        kept_target, following, field, kernel, kept_table
    )
    received = exchanged(sent, range(last))
    wrapped, *received = lax.optimization_barrier((wrapped, *received))
    mine, *sent = call(
        functools.partial(cross_last_kernel, count), slabs, [VMEM] * 6, PAIR_SCRATCH, "cross_last", aliases={5: 0}
    )(last_target, wrapped, last_field, last_kernel, last_table, mine)
    for piece in received + exchanged(sent, [last]):
        mine = mine + piece.astype(jnp.float32)
    return mine[None]


def solution(mesh):
    in_specs = (P("band", None, None), P(("band", "group"), None, None), P(("band", "group")), P())
    out_specs = P("band", "group", None)
    return jax.shard_map(shards, mesh=mesh, in_specs=in_specs, out_specs=out_specs, check_vma=False)
```

```python
import functools

import jax
import jax.numpy as jnp
import numpy as np
from jax import lax
from jax.experimental import pallas as pl
from jax.experimental.pallas import tpu as pltpu
from jax.sharding import PartitionSpec as P

SCREEN_SQUARE = 16.0
N = 64
HALF = 32
LANES = 128
WIDE = 256
BLOCKS = N * N // WIDE
STRIDE = 65
CHUNK = 256
MEMBERS = 4
SLAB = N // MEMBERS
PACKED = N * N + LANES
PACK_COPIES = 4
LATE = 2

DIAG, CAS, CAS_ROWS, CAS_COLS, EVEN_FIRST, TABLE_ROWS = 0, 256, 320, 384, 448, 512


def tables():
    k = np.arange(N)
    angle = (k[:, None] * k[None, :] % N).astype(np.float64) * (2.0 * np.pi / N)
    h = (np.cos(angle) + np.sin(angle)) / np.sqrt(float(N))
    order = np.concatenate([np.arange(0, N, 2), np.arange(1, N, 2)])
    table = np.zeros((TABLE_ROWS, WIDE))
    table[DIAG:CAS] = np.kron(np.eye(WIDE // N), h)
    table[CAS:CAS_ROWS, :N] = h
    table[CAS_ROWS:CAS_COLS, :N] = h[order]
    table[CAS_COLS:EVEN_FIRST, :N] = h[:, order]
    table[EVEN_FIRST:, :N] = np.eye(N)[order]
    return jnp.asarray(table, jnp.bfloat16)


def dot(a, b):
    return jnp.dot(a, b, preferred_element_type=jnp.float32)


def low_lanes():
    return lax.broadcasted_iota(jnp.int32, (HALF, LANES), 1) < N


def exchange(top, bottom, low):
    return (
        jnp.where(low, top, pltpu.roll(bottom, N, 1)),
        jnp.where(low, pltpu.roll(top, N, 1), bottom),
    )


def scatter_rows(block, column, turned, low):
    first, second = exchange(block[:HALF], block[HALF:], low)
    turned[pl.ds(2 * column, HALF, stride=STRIDE), :] = first
    turned[pl.ds(2 * column + 1, HALF, stride=STRIDE), :] = second


def gather_rows(column, turned, low):
    first = turned[pl.ds(2 * column, HALF, stride=STRIDE), :]
    second = turned[pl.ds(2 * column + 1, HALF, stride=STRIDE), :]
    top, bottom = exchange(first, second, low)
    return jnp.concatenate([top, bottom], axis=0)


def turned_block(block, turned):
    return jnp.concatenate(
        [turned[pl.ds((2 * block + part) * STRIDE, N), :].astype(jnp.bfloat16) for part in range(2)], axis=1
    )


def columns_of(block):
    return slice(block * WIDE, (block + 1) * WIDE)


def by_owner(me, ref, columns):
    return jnp.concatenate([ref[pl.ds((me ^ k) * SLAB, SLAB), columns] for k in range(MEMBERS)], axis=0)


def pair_field(me, target, source, scale, kernel_ready, table, turned, rows, emit):
    low = low_lanes()
    h_diag, h, h_rows = table[DIAG:CAS, :], table[CAS:CAS_ROWS, :N], table[CAS_ROWS:CAS_COLS, :N]
    for block in range(BLOCKS):
        first = dot(h_rows, target[:, columns_of(block)] * source[:, columns_of(block)])
        for part in range(2):
            scatter_rows(first[:, part * LANES : (part + 1) * LANES], 2 * block + part, turned, low)
    for block in range(BLOCKS):
        rows[block * N : (block + 1) * N, :] = dot(h, turned_block(block, turned)).astype(jnp.bfloat16)
    kernel = kernel_ready()
    for chunk in range(BLOCKS * N // CHUNK):
        part = slice(chunk * CHUNK, (chunk + 1) * CHUNK)
        spectrum = dot(rows[part, :], h_diag) * kernel[part, :]
        rows[part, :] = dot(spectrum.astype(jnp.bfloat16), h_diag).astype(jnp.bfloat16)
    for block in range(BLOCKS):
        back = dot(h, rows[block * N : (block + 1) * N, :])
        for part in range(2):
            turned[pl.ds((2 * block + part) * STRIDE, N), :] = back[:, part * LANES : (part + 1) * LANES]
    h_cols = by_owner(me, table.at[CAS_COLS:EVEN_FIRST], slice(0, N))
    for block in range(BLOCKS):
        back = jnp.concatenate(
            [gather_rows(2 * block + part, turned, low) for part in range(2)], axis=1
        ).astype(jnp.bfloat16)
        potential = dot(h_cols, back)
        emit(block, potential * scale * by_owner(me, source, columns_of(block)).astype(jnp.float32))


def on_late_band():
    return lax.axis_index("band") >= lax.axis_size("band") - LATE


def pack_kernel(label, source, packed, sems):
    step = N * N // PACK_COPIES
    copies = [
        pltpu.make_async_copy(
            source.at[:, i * step : (i + 1) * step], packed.at[:, i * step : (i + 1) * step], sems.at[i]
        )
        for i in range(PACK_COPIES)
    ]
    for copy in copies:
        copy.start()
    for half, part in enumerate((label[0] // 8, label[0] % 8)):
        packed[half * HALF : (half + 1) * HALF, N * N :] = (
            jnp.full((HALF, LANES), part, jnp.int32).astype(jnp.float32).astype(jnp.bfloat16)
        )
    for copy in copies:
        copy.wait()


def minus_occupation(count, packed):
    high, low = (packed[half * HALF : half * HALF + 16, N * N :].astype(jnp.float32) for half in range(2))
    shifted = (8.0 * high + low - count / 2.0) / (count / 4.0)
    return (-1.0 / (1.0 + jnp.exp(shifted)))[:1, :1]


def own_body(count, target, packed, mask, table, field, kernel, target_in, table_in, mask_in, turned, rows, sems):
    copies = [
        pltpu.make_async_copy(a, b, sems.at[i])
        for i, (a, b) in enumerate(((target, target_in), (table, table_in), (mask, mask_in)))
    ]
    for copy in copies:
        copy.start()
    me = lax.axis_index("group")
    low = low_lanes()
    ky = lax.broadcasted_iota(jnp.int32, (N, LANES), 0)
    lane = lax.broadcasted_iota(jnp.int32, (N, LANES), 1)

    def squared(k):
        signed = jnp.where(k < N // 2, k, k - N)
        return signed * signed

    plane = squared(ky) + squared(lane % N)
    for copy in copies:
        copy.wait()
    even_first = table_in[EVEN_FIRST:, :N]
    for block in range(BLOCKS):
        kept = dot(even_first, mask_in[:, columns_of(block)].astype(jnp.float32).astype(jnp.bfloat16))
        for part in range(2):
            scatter_rows(kept[:, part * LANES : (part + 1) * LANES], 2 * block + part, turned, low)
    for half in range(HALF):
        q_square = plane + squared(2 * half + lane // N)
        kept = turned[pl.ds(half * STRIDE, N), :]
        block, part = half // 2, half % 2
        kernel[block * N : (block + 1) * N, part * LANES : (part + 1) * LANES] = (
            kept * SCREEN_SQUARE / (q_square.astype(jnp.float32) + SCREEN_SQUARE)
        )

    def emit(block, value):
        field[:, columns_of(block)] = value

    pair_field(me, target_in, packed, minus_occupation(count, packed), lambda: kernel, table_in, turned, rows, emit)


def own_kernel(count, *refs):
    @pl.when(jnp.logical_not(on_late_band()))
    def _():
        own_body(count, *refs)


def own_late_kernel(count, *refs):
    @pl.when(on_late_band())
    def _():
        own_body(count, *refs)


def cross_body(count, target, packed, field, kernel, table, mine, sent, scratch):
    def emit(block, value):
        total = field[:, columns_of(block)] + value
        mine[:, columns_of(block)] = total[:SLAB]
        for k in range(1, MEMBERS):
            sent[k - 1][:, columns_of(block)] = total[k * SLAB : (k + 1) * SLAB].astype(jnp.bfloat16)

    pair_field(
        lax.axis_index("group"), target, packed, minus_occupation(count, packed), lambda: kernel, table, *scratch, emit
    )


def cross_kernel(count, target, packed, field, kernel, table, mine, *rest):
    @pl.when(jnp.logical_not(on_late_band()))
    def _():
        cross_body(count, target, packed, field, kernel, table, mine, rest[: MEMBERS - 1], rest[MEMBERS - 1 :])


def cross_late_kernel(count, target, packed, field, kernel, table, held, mine, *rest):
    @pl.when(on_late_band())
    def _():
        cross_body(count, target, packed, field, kernel, table, mine, rest[: MEMBERS - 1], rest[MEMBERS - 1 :])

    @pl.when(jnp.logical_not(on_late_band()))
    def _():
        mine[...] = held[...]


def shape(rows, columns, dtype):
    return jax.ShapeDtypeStruct((rows, columns), dtype)


PAIR_SCRATCH = [pltpu.VMEM((HALF * STRIDE, LANES), jnp.float32), pltpu.VMEM((BLOCKS * N, WIDE), jnp.bfloat16)]
OWN_SCRATCH = [pltpu.VMEM((N, N * N), jnp.int32)] + PAIR_SCRATCH + [pltpu.SemaphoreType.DMA((3,))]
VMEM = pl.BlockSpec(memory_space=pltpu.VMEM)
HBM = pl.BlockSpec(memory_space=pltpu.HBM)


def call(kernel, outs, in_specs, scratch, name, aliases=None, flops=6 * 2 * N**4):
    return pl.pallas_call(
        kernel,
        out_shape=outs,
        in_specs=in_specs,
        out_specs=[VMEM] * len(outs),
        scratch_shapes=scratch,
        input_output_aliases=aliases or {},
        compiler_params=pltpu.CompilerParams(vmem_limit_bytes=40 * 1024 * 1024),
        cost_estimate=pl.CostEstimate(flops=flops, bytes_accessed=4 * 1024 * 1024, transcendentals=0),
        name=name,
    )


def in_hbm(value):
    return pltpu.with_memory_space_constraint(value, pltpu.HBM)


def sent_along(value, pairs):
    return lax.ppermute(value, ("band", "group"), [(s[0] * MEMBERS + s[1], t[0] * MEMBERS + t[1]) for s, t in pairs])


def exchanged(sent, bands):
    return [
        sent_along(sent[bits - 1], [((b, g), (b, g ^ bits)) for b in bands for g in range(MEMBERS)]) for bits in (2, 3, 1)
    ]


def shards(trial, orbitals, labels, kernel_mask):
    bands = lax.axis_size("band")
    count = bands * MEMBERS
    last = bands - 1
    members = range(MEMBERS)
    target, table, mask = in_hbm(trial[0]), in_hbm(tables()), in_hbm(kernel_mask)
    packed = call(
        pack_kernel,
        [shape(N, PACKED, jnp.bfloat16)],
        [pl.BlockSpec(memory_space=pltpu.SMEM), HBM],
        [pltpu.SemaphoreType.DMA((PACK_COPIES,))],
        "pack",
        flops=0,
    )(labels, in_hbm(orbitals[0]))[0]
    following = sent_along(packed, [((b, g), (b - 1, g)) for b in range(1, last) for g in members])
    planes = [
        shape(N, N * N, jnp.float32),
        shape(BLOCKS * N, WIDE, jnp.float32),
        shape(N, N * N, jnp.bfloat16),
        shape(TABLE_ROWS, WIDE, jnp.bfloat16),
    ]
    sources = [HBM, VMEM, HBM, HBM]
    field, kernel, kept_target, kept_table = call(
        functools.partial(own_kernel, count), planes, sources, OWN_SCRATCH, "own"
    )(target, packed, mask, table)
    packed, field = lax.optimization_barrier((packed, field))
    wrapped = sent_along(packed, [((s, g), (t, g)) for s, t in ((0, last), (last, last - 1)) for g in members])
    late_field, late_kernel, late_target, late_table = call(
        functools.partial(own_late_kernel, count), planes, sources, OWN_SCRATCH, "own_late"
    )(target, packed, mask, table)
    slabs = [shape(SLAB, N * N, jnp.float32)] + [shape(SLAB, N * N, jnp.bfloat16)] * (MEMBERS - 1)
    mine, *sent = call(functools.partial(cross_kernel, count), slabs, [VMEM] * 5, PAIR_SCRATCH, "cross")(
        kept_target, following, field, kernel, kept_table
    )
    received = exchanged(sent, range(bands - LATE))
    mine, *sent = call(
        functools.partial(cross_late_kernel, count), slabs, [VMEM] * 6, PAIR_SCRATCH, "cross_late", aliases={5: 0}
    )(late_target, wrapped, late_field, late_kernel, late_table, mine)
    for piece in received + exchanged(sent, range(bands - LATE, bands)):
        mine = mine + piece.astype(jnp.float32)
    return mine[None]


def solution(mesh):
    in_specs = (P("band", None, None), P(("band", "group"), None, None), P(("band", "group")), P())
    out_specs = P("band", "group", None)
    return jax.shard_map(shards, mesh=mesh, in_specs=in_specs, out_specs=out_specs, check_vma=False)
```

```python
import functools

import jax
import jax.numpy as jnp
import numpy as np
from jax import lax
from jax.experimental import pallas as pl
from jax.experimental.pallas import tpu as pltpu
from jax.sharding import PartitionSpec as P

SCREEN_SQUARE = 16.0
N = 64
HALF = 32
LANES = 128
WIDE = 256
BLOCKS = N * N // WIDE
STRIDE = 65
CHUNK = 256
MEMBERS = 4
SLAB = N // MEMBERS
PACKED = N * N + LANES
PACK_COPIES = 4
LATE = 2
ROW = 8

DIAG, CAS, CAS_ROWS, CAS_COLS, EVEN_FIRST, TABLE_ROWS = 0, 256, 320, 384, 448, 512


def tables():
    k = np.arange(N)
    angle = (k[:, None] * k[None, :] % N).astype(np.float64) * (2.0 * np.pi / N)
    h = (np.cos(angle) + np.sin(angle)) / np.sqrt(float(N))
    order = np.concatenate([np.arange(0, N, 2), np.arange(1, N, 2)])
    table = np.zeros((TABLE_ROWS, WIDE))
    table[DIAG:CAS] = np.kron(np.eye(WIDE // N), h)
    table[CAS:CAS_ROWS, :N] = h
    table[CAS_ROWS:CAS_COLS, :N] = h[order]
    table[CAS_COLS:EVEN_FIRST, :N] = h[:, order]
    table[EVEN_FIRST:, :N] = np.eye(N)[order]
    return jnp.asarray(table, jnp.bfloat16)


def dot(a, b):
    return jnp.dot(a, b, preferred_element_type=jnp.float32)


def low_lanes():
    return lax.broadcasted_iota(jnp.int32, (HALF, LANES), 1) < N


def exchange(top, bottom, low):
    return (
        jnp.where(low, top, pltpu.roll(bottom, N, 1)),
        jnp.where(low, pltpu.roll(top, N, 1), bottom),
    )


def scatter_rows(block, column, turned, low):
    first, second = exchange(block[:HALF], block[HALF:], low)
    turned[pl.ds(2 * column, HALF, stride=STRIDE), :] = first
    turned[pl.ds(2 * column + 1, HALF, stride=STRIDE), :] = second


def gather_rows(column, turned, low):
    first = turned[pl.ds(2 * column, HALF, stride=STRIDE), :]
    second = turned[pl.ds(2 * column + 1, HALF, stride=STRIDE), :]
    top, bottom = exchange(first, second, low)
    return jnp.concatenate([top, bottom], axis=0)


def turned_block(block, turned):
    return jnp.concatenate(
        [turned[pl.ds((2 * block + part) * STRIDE, N), :].astype(jnp.bfloat16) for part in range(2)], axis=1
    )


def columns_of(block):
    return slice(block * WIDE, (block + 1) * WIDE)


def by_owner(me, ref, columns):
    return jnp.concatenate([ref[pl.ds((me ^ k) * SLAB, SLAB), columns] for k in range(MEMBERS)], axis=0)


def pair_field(me, target, source, scale, kernel_ready, table, turned, rows, emit):
    low = low_lanes()
    h_diag, h, h_rows = table[DIAG:CAS, :], table[CAS:CAS_ROWS, :N], table[CAS_ROWS:CAS_COLS, :N]
    for block in range(BLOCKS):
        first = dot(h_rows, target[:, columns_of(block)] * source[:, columns_of(block)])
        for part in range(2):
            scatter_rows(first[:, part * LANES : (part + 1) * LANES], 2 * block + part, turned, low)
    for block in range(BLOCKS):
        rows[block * N : (block + 1) * N, :] = dot(h, turned_block(block, turned)).astype(jnp.bfloat16)
    kernel = kernel_ready()
    for chunk in range(BLOCKS * N // CHUNK):
        part = slice(chunk * CHUNK, (chunk + 1) * CHUNK)
        spectrum = dot(rows[part, :], h_diag) * kernel[part, :]
        rows[part, :] = dot(spectrum.astype(jnp.bfloat16), h_diag).astype(jnp.bfloat16)
    for block in range(BLOCKS):
        back = dot(h, rows[block * N : (block + 1) * N, :])
        for part in range(2):
            turned[pl.ds((2 * block + part) * STRIDE, N), :] = back[:, part * LANES : (part + 1) * LANES]
    h_cols = by_owner(me, table.at[CAS_COLS:EVEN_FIRST], slice(0, N))
    for block in range(BLOCKS):
        back = jnp.concatenate(
            [gather_rows(2 * block + part, turned, low) for part in range(2)], axis=1
        ).astype(jnp.bfloat16)
        potential = dot(h_cols, back)
        emit(block, potential * scale * by_owner(me, source, columns_of(block)).astype(jnp.float32))


def on_late_band():
    return lax.axis_index("band") >= lax.axis_size("band") - LATE


def pack_kernel(label, source, packed, sems):
    step = N * N // PACK_COPIES
    copies = [
        pltpu.make_async_copy(
            source.at[:, i * step : (i + 1) * step], packed.at[:, i * step : (i + 1) * step], sems.at[i]
        )
        for i in range(PACK_COPIES)
    ]
    for copy in copies:
        copy.start()
    for half, part in enumerate((label[0] // 8, label[0] % 8)):
        packed[half * HALF : (half + 1) * HALF, N * N :] = (
            jnp.full((HALF, LANES), part, jnp.int32).astype(jnp.float32).astype(jnp.bfloat16)
        )
    for copy in copies:
        copy.wait()


def minus_occupation(count, packed):
    high, low = (packed[half * HALF : half * HALF + 16, N * N :].astype(jnp.float32) for half in range(2))
    shifted = (8.0 * high + low - count / 2.0) / (count / 4.0)
    return (-1.0 / (1.0 + jnp.exp(shifted)))[:1, :1]


def own_body(count, target, packed, mask, table, field, kernel, target_in, table_in, mask_in, turned, rows, sems):
    copies = [
        pltpu.make_async_copy(a, b, sems.at[i])
        for i, (a, b) in enumerate(((target, target_in), (table, table_in), (mask, mask_in)))
    ]
    for copy in copies:
        copy.start()
    me = lax.axis_index("group")
    low = low_lanes()
    ky = lax.broadcasted_iota(jnp.int32, (N, LANES), 0)
    lane = lax.broadcasted_iota(jnp.int32, (N, LANES), 1)

    def squared(k):
        signed = jnp.where(k < N // 2, k, k - N)
        return signed * signed

    plane = squared(ky) + squared(lane % N)
    for copy in copies:
        copy.wait()
    even_first = table_in[EVEN_FIRST:, :N]
    for block in range(BLOCKS):
        kept = dot(even_first, mask_in[:, columns_of(block)].astype(jnp.float32).astype(jnp.bfloat16))
        for part in range(2):
            scatter_rows(kept[:, part * LANES : (part + 1) * LANES], 2 * block + part, turned, low)
    for half in range(HALF):
        q_square = plane + squared(2 * half + lane // N)
        kept = turned[pl.ds(half * STRIDE, N), :]
        block, part = half // 2, half % 2
        kernel[block * N : (block + 1) * N, part * LANES : (part + 1) * LANES] = (
            kept * SCREEN_SQUARE / (q_square.astype(jnp.float32) + SCREEN_SQUARE)
        )

    def emit(block, value):
        field[:, columns_of(block)] = value

    pair_field(me, target_in, packed, minus_occupation(count, packed), lambda: kernel, table_in, turned, rows, emit)


def own_kernel(count, *refs):
    @pl.when(jnp.logical_not(on_late_band()))
    def _():
        own_body(count, *refs)


def own_late_kernel(count, *refs):
    @pl.when(on_late_band())
    def _():
        own_body(count, *refs)


def cross_body(count, target, packed, field, kernel, table, mine, sent, scratch):
    def emit(block, value):
        total = field[:, columns_of(block)] + value
        mine[:, columns_of(block)] = total[:SLAB]
        for k in range(1, MEMBERS):
            sent[k - 1][:, columns_of(block)] = total[k * SLAB : (k + 1) * SLAB].astype(jnp.bfloat16)

    pair_field(
        lax.axis_index("group"), target, packed, minus_occupation(count, packed), lambda: kernel, table, *scratch, emit
    )


def cross_kernel(count, target, packed, field, kernel, table, mine, *rest):
    @pl.when(jnp.logical_not(on_late_band()))
    def _():
        cross_body(count, target, packed, field, kernel, table, mine, rest[: MEMBERS - 1], rest[MEMBERS - 1 :])


def cross_late_kernel(count, target, packed, field, kernel, table, held, mine, *rest):
    @pl.when(on_late_band())
    def _():
        cross_body(count, target, packed, field, kernel, table, mine, rest[: MEMBERS - 1], rest[MEMBERS - 1 :])

    @pl.when(jnp.logical_not(on_late_band()))
    def _():
        mine[...] = held[...]


def shape(rows, columns, dtype):
    return jax.ShapeDtypeStruct((rows, columns), dtype)


PAIR_SCRATCH = [pltpu.VMEM((HALF * STRIDE, LANES), jnp.float32), pltpu.VMEM((BLOCKS * N, WIDE), jnp.bfloat16)]
OWN_SCRATCH = [pltpu.VMEM((N, N * N), jnp.int32)] + PAIR_SCRATCH + [pltpu.SemaphoreType.DMA((3,))]
VMEM = pl.BlockSpec(memory_space=pltpu.VMEM)
HBM = pl.BlockSpec(memory_space=pltpu.HBM)


def call(kernel, outs, in_specs, scratch, name, aliases=None, flops=6 * 2 * N**4):
    return pl.pallas_call(
        kernel,
        out_shape=outs,
        in_specs=in_specs,
        out_specs=[VMEM] * len(outs),
        scratch_shapes=scratch,
        input_output_aliases=aliases or {},
        compiler_params=pltpu.CompilerParams(vmem_limit_bytes=40 * 1024 * 1024),
        cost_estimate=pl.CostEstimate(flops=flops, bytes_accessed=4 * 1024 * 1024, transcendentals=0),
        name=name,
    )


def in_hbm(value):
    return pltpu.with_memory_space_constraint(value, pltpu.HBM)


def sent_along(value, pairs):
    return lax.ppermute(value, ("band", "group"), [(s[0] * MEMBERS + s[1], t[0] * MEMBERS + t[1]) for s, t in pairs])


def next_sources(bands):
    count = lax.axis_size("band")
    return [((b, g), ((b - 1) % count, g ^ 2 if b % ROW == 0 else g)) for b in bands for g in range(MEMBERS)]


def exchanged(sent, bands):
    return [
        sent_along(sent[bits - 1], [((b, g), (b, g ^ bits)) for b in bands for g in range(MEMBERS)]) for bits in (2, 3, 1)
    ]


def shards(trial, orbitals, labels, kernel_mask):
    bands = lax.axis_size("band")
    count = bands * MEMBERS
    target, table, mask = in_hbm(trial[0]), in_hbm(tables()), in_hbm(kernel_mask)
    packed = call(
        pack_kernel,
        [shape(N, PACKED, jnp.bfloat16)],
        [pl.BlockSpec(memory_space=pltpu.SMEM), HBM],
        [pltpu.SemaphoreType.DMA((PACK_COPIES,))],
        "pack",
        flops=0,
    )(labels, in_hbm(orbitals[0]))[0]
    following = sent_along(packed, next_sources(range(1, bands - 1)))
    planes = [
        shape(N, N * N, jnp.float32),
        shape(BLOCKS * N, WIDE, jnp.float32),
        shape(N, N * N, jnp.bfloat16),
        shape(TABLE_ROWS, WIDE, jnp.bfloat16),
    ]
    sources = [HBM, VMEM, HBM, HBM]
    field, kernel, kept_target, kept_table = call(
        functools.partial(own_kernel, count), planes, sources, OWN_SCRATCH, "own"
    )(target, packed, mask, table)
    packed, field = lax.optimization_barrier((packed, field))
    wrapped = sent_along(packed, next_sources((0, bands - 1)))
    late_field, late_kernel, late_target, late_table = call(
        functools.partial(own_late_kernel, count), planes, sources, OWN_SCRATCH, "own_late"
    )(target, packed, mask, table)
    slabs = [shape(SLAB, N * N, jnp.float32)] + [shape(SLAB, N * N, jnp.bfloat16)] * (MEMBERS - 1)
    mine, *sent = call(functools.partial(cross_kernel, count), slabs, [VMEM] * 5, PAIR_SCRATCH, "cross")(
        kept_target, following, field, kernel, kept_table
    )
    received = exchanged(sent, range(bands - LATE))
    mine, *sent = call(
        functools.partial(cross_late_kernel, count), slabs, [VMEM] * 6, PAIR_SCRATCH, "cross_late", aliases={5: 0}
    )(late_target, wrapped, late_field, late_kernel, late_table, mine)
    for piece in received + exchanged(sent, range(bands - LATE, bands)):
        mine = mine + piece.astype(jnp.float32)
    return mine[None]


def solution(mesh):
    in_specs = (P("band", None, None), P(("band", "group"), None, None), P(("band", "group")), P())
    out_specs = P("band", "group", None)
    return jax.shard_map(shards, mesh=mesh, in_specs=in_specs, out_specs=out_specs, check_vma=False)
```

```python
import functools

import jax
import jax.numpy as jnp
import numpy as np
from jax import lax
from jax.experimental import pallas as pl
from jax.experimental.pallas import tpu as pltpu
from jax.sharding import PartitionSpec as P


SCREEN_SQUARE = 16.0
N = 64
HALF = 32
LANES = 128
WIDE = 256
BLOCKS = N * N // WIDE
STRIDE = 65
TURNED_ROWS = HALF * STRIDE + N + 8
CHUNK = 256
MEMBERS = 4
SLAB = N // MEMBERS
PACKED = N * N + LANES
PACK_COPIES = 4
LATE = 2
ROW = 8

DIAG, CAS, CAS_ROWS, CAS_COLS, EVEN_FIRST, TABLE_ROWS = 0, 256, 320, 384, 448, 512


def tables():
    k = np.arange(N)
    angle = (k[:, None] * k[None, :] % N).astype(np.float64) * (2.0 * np.pi / N)
    h = (np.cos(angle) + np.sin(angle)) / np.sqrt(float(N))
    order = np.concatenate([np.arange(0, N, 2), np.arange(1, N, 2)])
    table = np.zeros((TABLE_ROWS, WIDE))
    table[DIAG:CAS] = np.kron(np.eye(WIDE // N), h)
    table[CAS:CAS_ROWS, :N] = h
    table[CAS_ROWS:CAS_COLS, :N] = h[order]
    table[CAS_COLS:EVEN_FIRST, :N] = h[:, order]
    table[EVEN_FIRST:, :N] = np.eye(N)[order]
    return jnp.asarray(table, jnp.bfloat16)


def dot(a, b):
    return jnp.dot(a, b, preferred_element_type=jnp.float32)


def low_lanes():
    return lax.broadcasted_iota(jnp.int32, (HALF, LANES), 1) < N


def exchange(top, bottom, low):
    return (
        jnp.where(low, top, pltpu.roll(bottom, N, 1)),
        jnp.where(low, pltpu.roll(top, N, 1), bottom),
    )


def scatter_rows(block, column, turned, low):
    first, second = exchange(block[:HALF], block[HALF:], low)
    turned[pl.ds(2 * column, HALF, stride=STRIDE), :] = first
    turned[pl.ds(2 * column + 1, HALF, stride=STRIDE), :] = second


def gather_rows(column, turned, low):
    first = turned[pl.ds(2 * column, HALF, stride=STRIDE), :]
    second = turned[pl.ds(2 * column + 1, HALF, stride=STRIDE), :]
    top, bottom = exchange(first, second, low)
    return jnp.concatenate([top, bottom], axis=0)


def turned_block(block, turned):
    return jnp.concatenate(
        [turned[pl.ds((2 * block + part) * STRIDE, N), :].astype(jnp.bfloat16) for part in range(2)], axis=1
    )


def columns_of(block):
    return slice(block * WIDE, (block + 1) * WIDE)


def by_owner(me, ref, columns):
    return jnp.concatenate([ref[pl.ds((me ^ k) * SLAB, SLAB), columns] for k in range(MEMBERS)], axis=0)


def pair_field(me, target, source, scale, kernel_ready, table, turned, rows, emit):
    low = low_lanes()
    h_diag, h, h_rows = table[DIAG:CAS, :], table[CAS:CAS_ROWS, :N], table[CAS_ROWS:CAS_COLS, :N]
    for block in range(BLOCKS):
        first = dot(h_rows, target[:, columns_of(block)] * source[:, columns_of(block)])
        for part in range(2):
            scatter_rows(first[:, part * LANES : (part + 1) * LANES], 2 * block + part, turned, low)
    for block in range(BLOCKS):
        rows[block * N : (block + 1) * N, :] = dot(h, turned_block(block, turned)).astype(jnp.bfloat16)
    kernel = kernel_ready()
    for chunk in range(BLOCKS * N // CHUNK):
        part = slice(chunk * CHUNK, (chunk + 1) * CHUNK)
        spectrum = dot(rows[part, :], h_diag) * kernel[part, :]
        rows[part, :] = dot(spectrum.astype(jnp.bfloat16), h_diag).astype(jnp.bfloat16)
    for block in range(BLOCKS):
        back = dot(h, rows[block * N : (block + 1) * N, :])
        for part in range(2):
            turned[pl.ds((2 * block + part) * STRIDE, N), :] = back[:, part * LANES : (part + 1) * LANES]
    h_cols = by_owner(me, table.at[CAS_COLS:EVEN_FIRST], slice(0, N))
    for block in range(BLOCKS):
        back = jnp.concatenate(
            [gather_rows(2 * block + part, turned, low) for part in range(2)], axis=1
        ).astype(jnp.bfloat16)
        potential = dot(h_cols, back)
        emit(block, potential * scale * by_owner(me, source, columns_of(block)).astype(jnp.float32))


def on_late_band():
    return lax.axis_index("band") >= lax.axis_size("band") - LATE


def pack_kernel(label, source, packed, sems):
    step = N * N // PACK_COPIES
    copies = [
        pltpu.make_async_copy(
            source.at[:, i * step : (i + 1) * step], packed.at[:, i * step : (i + 1) * step], sems.at[i]
        )
        for i in range(PACK_COPIES)
    ]
    for copy in copies:
        copy.start()
    for half, part in enumerate((label[0] // 8, label[0] % 8)):
        packed[half * HALF : (half + 1) * HALF, N * N :] = (
            jnp.full((HALF, LANES), part, jnp.int32).astype(jnp.float32).astype(jnp.bfloat16)
        )
    for copy in copies:
        copy.wait()


def minus_occupation(count, packed):
    high, low = (packed[half * HALF : half * HALF + 16, N * N :].astype(jnp.float32) for half in range(2))
    shifted = (8.0 * high + low - count / 2.0) / (count / 4.0)
    return (-1.0 / (1.0 + jnp.exp(shifted)))[:1, :1]


def own_body(count, target, packed, mask, table, field, kernel, target_in, table_in, mask_in, turned, rows, sems):
    copies = [
        pltpu.make_async_copy(a, b, sems.at[i])
        for i, (a, b) in enumerate(((target, target_in), (table, table_in), (mask, mask_in)))
    ]
    for copy in copies:
        copy.start()
    me = lax.axis_index("group")
    low = low_lanes()
    ky = lax.broadcasted_iota(jnp.int32, (N, LANES), 0)
    lane = lax.broadcasted_iota(jnp.int32, (N, LANES), 1)

    def squared(k):
        signed = jnp.where(k < N // 2, k, k - N)
        return signed * signed

    plane = squared(ky) + squared(lane % N)
    for copy in copies:
        copy.wait()
    even_first = table_in[EVEN_FIRST:, :N]
    for block in range(BLOCKS):
        kept = dot(even_first, mask_in[:, columns_of(block)].astype(jnp.float32).astype(jnp.bfloat16))
        for part in range(2):
            scatter_rows(kept[:, part * LANES : (part + 1) * LANES], 2 * block + part, turned, low)
    for half in range(HALF):
        q_square = plane + squared(2 * half + lane // N)
        kept = turned[pl.ds(half * STRIDE, N), :]
        block, part = half // 2, half % 2
        kernel[block * N : (block + 1) * N, part * LANES : (part + 1) * LANES] = (
            kept * SCREEN_SQUARE / (q_square.astype(jnp.float32) + SCREEN_SQUARE)
        )

    def emit(block, value):
        field[:, columns_of(block)] = value

    pair_field(me, target_in, packed, minus_occupation(count, packed), lambda: kernel, table_in, turned, rows, emit)


def own_kernel(count, *refs):
    @pl.when(jnp.logical_not(on_late_band()))
    def _():
        own_body(count, *refs)


def own_late_kernel(count, *refs):
    @pl.when(on_late_band())
    def _():
        own_body(count, *refs)


def cross_body(count, target, packed, field, kernel, table, scratch, emit_total):
    def emit(block, value):
        emit_total(columns_of(block), field[:, columns_of(block)] + value)

    pair_field(
        lax.axis_index("group"), target, packed, minus_occupation(count, packed), lambda: kernel, table, *scratch, emit
    )


def slab(total, k):
    return total[k * SLAB : (k + 1) * SLAB]


def cross_kernel(count, target, packed, field, kernel, table, mine, *rest):
    sent, scratch = rest[: MEMBERS - 1], rest[MEMBERS - 1 :]

    def emit_total(columns, total):
        mine[:, columns] = slab(total, 0)
        for k in range(1, MEMBERS):
            sent[k - 1][:, columns] = slab(total, k).astype(jnp.bfloat16)

    @pl.when(jnp.logical_not(on_late_band()))
    def _():
        cross_body(count, target, packed, field, kernel, table, scratch, emit_total)


def cross_late_kernel(count, target, packed, field, kernel, table, held, mine, kept, sent, *scratch):
    def emit_total(columns, total):
        mine[:, columns] = slab(total, 0)
        kept[:, columns] = slab(total, 2)
        sent[:SLAB, columns] = slab(total, 1).astype(jnp.bfloat16)
        sent[SLAB:, columns] = slab(total, 3).astype(jnp.bfloat16)

    @pl.when(on_late_band())
    def _():
        cross_body(count, target, packed, field, kernel, table, scratch, emit_total)

    @pl.when(jnp.logical_not(on_late_band()))
    def _():
        mine[...] = held[...]


def chip_sum_kernel(kept, got, sent):
    @pl.when(on_late_band())
    def _():
        sent[...] = (kept[...] + got[SLAB:, :].astype(jnp.float32)).astype(jnp.bfloat16)


def shape(rows, columns, dtype):
    return jax.ShapeDtypeStruct((rows, columns), dtype)


PAIR_SCRATCH = [pltpu.VMEM((TURNED_ROWS, LANES), jnp.float32), pltpu.VMEM((BLOCKS * N, WIDE), jnp.bfloat16)]
OWN_SCRATCH = [pltpu.VMEM((N, N * N), jnp.int32)] + PAIR_SCRATCH + [pltpu.SemaphoreType.DMA((3,))]
VMEM = pl.BlockSpec(memory_space=pltpu.VMEM)
HBM = pl.BlockSpec(memory_space=pltpu.HBM)


def call(kernel, outs, in_specs, scratch, aliases=None, flops=6 * 2 * N**4):
    return pl.pallas_call(
        kernel,
        out_shape=outs,
        in_specs=in_specs,
        out_specs=[VMEM] * len(outs),
        scratch_shapes=scratch,
        input_output_aliases=aliases or {},
        compiler_params=pltpu.CompilerParams(vmem_limit_bytes=40 * 1024 * 1024),
        cost_estimate=pl.CostEstimate(flops=flops, bytes_accessed=4 * 1024 * 1024, transcendentals=0),
    )


def in_hbm(value):
    return pltpu.with_memory_space_constraint(value, pltpu.HBM)


def sent_along(value, pairs):
    return lax.ppermute(value, ("band", "group"), [(s[0] * MEMBERS + s[1], t[0] * MEMBERS + t[1]) for s, t in pairs])


def next_sources(bands):
    count = lax.axis_size("band")
    return [((b, g), ((b - 1) % count, g ^ 2 if b % ROW == 0 else g)) for b in bands for g in range(MEMBERS)]


def swapped(value, bits, bands):
    return sent_along(value, [((b, g), (b, g ^ bits)) for b in bands for g in range(MEMBERS)])


def shards(trial, orbitals, labels, kernel_mask):
    bands = lax.axis_size("band")
    count = bands * MEMBERS
    target, table, mask = in_hbm(trial[0]), in_hbm(tables()), in_hbm(kernel_mask)
    packed = call(
        pack_kernel,
        [shape(N, PACKED, jnp.bfloat16)],
        [pl.BlockSpec(memory_space=pltpu.SMEM), HBM],
        [pltpu.SemaphoreType.DMA((PACK_COPIES,))],
        flops=0,
    )(labels, in_hbm(orbitals[0]))[0]
    following = sent_along(packed, next_sources(range(1, bands - 1)))
    planes = [
        shape(N, N * N, jnp.float32),
        shape(BLOCKS * N, WIDE, jnp.float32),
        shape(N, N * N, jnp.bfloat16),
        shape(TABLE_ROWS, WIDE, jnp.bfloat16),
    ]
    sources = [HBM, VMEM, HBM, HBM]
    field, kernel, kept_target, kept_table = call(
        functools.partial(own_kernel, count), planes, sources, OWN_SCRATCH
    )(target, packed, mask, table)
    packed, field = lax.optimization_barrier((packed, field))
    wrapped = sent_along(packed, next_sources((0, bands - 1)))
    late_field, late_kernel, late_target, late_table = call(
        functools.partial(own_late_kernel, count), planes, sources, OWN_SCRATCH
    )(target, packed, mask, table)
    slabs = [shape(SLAB, N * N, jnp.float32)] + [shape(SLAB, N * N, jnp.bfloat16)] * (MEMBERS - 1)
    mine, *sent = call(functools.partial(cross_kernel, count), slabs, [VMEM] * 5, PAIR_SCRATCH)(
        kept_target, following, field, kernel, kept_table
    )
    received = []
    for bits in (2, 3, 1):
        received.append(swapped(sent[bits - 1], bits, range(bands - LATE)))
    late_bands = range(bands - LATE, bands)
    late_slabs = [shape(SLAB, N * N, jnp.float32)] * 2 + [shape(2 * SLAB, N * N, jnp.bfloat16)]
    mine, kept, sent = call(
        functools.partial(cross_late_kernel, count), late_slabs, [VMEM] * 6, PAIR_SCRATCH, aliases={5: 0}
    )(late_target, wrapped, late_field, late_kernel, late_table, mine)
    near = swapped(sent, 1, late_bands)
    far = call(chip_sum_kernel, [shape(SLAB, N * N, jnp.bfloat16)], [VMEM] * 2, [], flops=0)(kept, near)[0]
    for piece in received + [near[:SLAB], swapped(far, 2, late_bands)]:
        mine = mine + piece.astype(jnp.float32)
    return mine[None]


def solution(mesh):
    in_specs = (P("band", None, None), P(("band", "group"), None, None), P(("band", "group")), P())
    out_specs = P("band", "group", None)
    return jax.shard_map(shards, mesh=mesh, in_specs=in_specs, out_specs=out_specs, check_vma=False)
```

```python
import functools

import jax
import jax.numpy as jnp
import numpy as np
from jax import lax
from jax.experimental import pallas as pl
from jax.experimental.pallas import tpu as pltpu
from jax.sharding import PartitionSpec as P


SCREEN_SQUARE = 16.0
N = 64
HALF = 32
LANES = 128
WIDE = 256
BLOCKS = N * N // WIDE
STRIDE = 65
TURNED_ROWS = HALF * STRIDE + N + 8
CHUNK = 256
MEMBERS = 4
SLAB = N // MEMBERS
PACKED = N * N + LANES
PACK_COPIES = 4
LATE = 2
ROW = 8

DIAG, CAS, CAS_ROWS, CAS_COLS, EVEN_FIRST, TABLE_ROWS = 0, 256, 320, 384, 448, 512


def tables():
    k = np.arange(N)
    angle = (k[:, None] * k[None, :] % N).astype(np.float64) * (2.0 * np.pi / N)
    h = (np.cos(angle) + np.sin(angle)) / np.sqrt(float(N))
    order = np.concatenate([np.arange(0, N, 2), np.arange(1, N, 2)])
    table = np.zeros((TABLE_ROWS, WIDE))
    table[DIAG:CAS] = np.kron(np.eye(WIDE // N), h)
    table[CAS:CAS_ROWS, :N] = h
    table[CAS_ROWS:CAS_COLS, :N] = h[order]
    table[CAS_COLS:EVEN_FIRST, :N] = h[:, order]
    table[EVEN_FIRST:, :N] = np.eye(N)[order]
    return jnp.asarray(table, jnp.bfloat16)


def dot(a, b):
    return jnp.dot(a, b, preferred_element_type=jnp.float32)


def low_lanes():
    return lax.broadcasted_iota(jnp.int32, (HALF, LANES), 1) < N


def exchange(top, bottom, low):
    return (
        jnp.where(low, top, pltpu.roll(bottom, N, 1)),
        jnp.where(low, pltpu.roll(top, N, 1), bottom),
    )


def scatter_rows(block, column, turned, low):
    first, second = exchange(block[:HALF], block[HALF:], low)
    turned[pl.ds(2 * column, HALF, stride=STRIDE), :] = first
    turned[pl.ds(2 * column + 1, HALF, stride=STRIDE), :] = second


def gather_rows(column, turned, low):
    first = turned[pl.ds(2 * column, HALF, stride=STRIDE), :]
    second = turned[pl.ds(2 * column + 1, HALF, stride=STRIDE), :]
    top, bottom = exchange(first, second, low)
    return jnp.concatenate([top, bottom], axis=0)


def turned_block(block, turned):
    return jnp.concatenate(
        [turned[pl.ds((2 * block + part) * STRIDE, N), :].astype(jnp.bfloat16) for part in range(2)], axis=1
    )


def columns_of(block):
    return slice(block * WIDE, (block + 1) * WIDE)


def by_owner(me, ref, columns):
    return jnp.concatenate([ref[pl.ds((me ^ k) * SLAB, SLAB), columns] for k in range(MEMBERS)], axis=0)


def pair_field(me, target, source, scale, kernel_ready, table, turned, rows, emit):
    low = low_lanes()
    h_diag, h, h_rows = table[DIAG:CAS, :], table[CAS:CAS_ROWS, :N], table[CAS_ROWS:CAS_COLS, :N]
    for block in range(BLOCKS):
        first = dot(h_rows, target[:, columns_of(block)] * source[:, columns_of(block)])
        for part in range(2):
            scatter_rows(first[:, part * LANES : (part + 1) * LANES], 2 * block + part, turned, low)
    for block in range(BLOCKS):
        rows[block * N : (block + 1) * N, :] = dot(h, turned_block(block, turned)).astype(jnp.bfloat16)
    kernel = kernel_ready()
    for chunk in range(BLOCKS * N // CHUNK):
        part = slice(chunk * CHUNK, (chunk + 1) * CHUNK)
        spectrum = dot(rows[part, :], h_diag) * kernel[part, :]
        rows[part, :] = dot(spectrum.astype(jnp.bfloat16), h_diag).astype(jnp.bfloat16)
    for block in range(BLOCKS):
        back = dot(h, rows[block * N : (block + 1) * N, :])
        for part in range(2):
            turned[pl.ds((2 * block + part) * STRIDE, N), :] = back[:, part * LANES : (part + 1) * LANES]
    h_cols = by_owner(me, table.at[CAS_COLS:EVEN_FIRST], slice(0, N))
    for block in range(BLOCKS):
        back = jnp.concatenate(
            [gather_rows(2 * block + part, turned, low) for part in range(2)], axis=1
        ).astype(jnp.bfloat16)
        potential = dot(h_cols, back)
        emit(block, potential * scale * by_owner(me, source, columns_of(block)).astype(jnp.float32))


def on_last_band():
    return lax.axis_index("band") == lax.axis_size("band") - 1


def on_late_band():
    return lax.axis_index("band") >= lax.axis_size("band") - LATE


def pack_kernel(late, label, source, packed, sems):
    @pl.when(on_late_band() if late else jnp.logical_not(on_last_band()))
    def _():
        step = N * N // PACK_COPIES
        copies = [
            pltpu.make_async_copy(
                source.at[:, i * step : (i + 1) * step], packed.at[:, i * step : (i + 1) * step], sems.at[i]
            )
            for i in range(PACK_COPIES)
        ]
        for copy in copies:
            copy.start()
        for half, part in enumerate((label[0] // 8, label[0] % 8)):
            packed[half * HALF : (half + 1) * HALF, N * N :] = (
                jnp.full((HALF, LANES), part, jnp.int32).astype(jnp.float32).astype(jnp.bfloat16)
            )
        for copy in copies:
            copy.wait()


def minus_occupation(count, packed):
    high, low = (packed[half * HALF : half * HALF + 16, N * N :].astype(jnp.float32) for half in range(2))
    shifted = (8.0 * high + low - count / 2.0) / (count / 4.0)
    return (-1.0 / (1.0 + jnp.exp(shifted)))[:1, :1]


def own_body(count, target, packed, mask, table, field, kernel, target_in, table_in, mask_in, turned, rows, sems):
    copies = [
        pltpu.make_async_copy(a, b, sems.at[i])
        for i, (a, b) in enumerate(((target, target_in), (table, table_in), (mask, mask_in)))
    ]
    for copy in copies:
        copy.start()
    me = lax.axis_index("group")
    low = low_lanes()
    ky = lax.broadcasted_iota(jnp.int32, (N, LANES), 0)
    lane = lax.broadcasted_iota(jnp.int32, (N, LANES), 1)

    def squared(k):
        signed = jnp.where(k < N // 2, k, k - N)
        return signed * signed

    plane = squared(ky) + squared(lane % N)
    for copy in copies:
        copy.wait()
    even_first = table_in[EVEN_FIRST:, :N]
    for block in range(BLOCKS):
        kept = dot(even_first, mask_in[:, columns_of(block)].astype(jnp.float32).astype(jnp.bfloat16))
        for part in range(2):
            scatter_rows(kept[:, part * LANES : (part + 1) * LANES], 2 * block + part, turned, low)
    for half in range(HALF):
        q_square = plane + squared(2 * half + lane // N)
        kept = turned[pl.ds(half * STRIDE, N), :]
        block, part = half // 2, half % 2
        kernel[block * N : (block + 1) * N, part * LANES : (part + 1) * LANES] = (
            kept * SCREEN_SQUARE / (q_square.astype(jnp.float32) + SCREEN_SQUARE)
        )

    def emit(block, value):
        field[:, columns_of(block)] = value

    pair_field(me, target_in, packed, minus_occupation(count, packed), lambda: kernel, table_in, turned, rows, emit)


def own_kernel(count, *refs):
    @pl.when(jnp.logical_not(on_late_band()))
    def _():
        own_body(count, *refs)


def own_late_kernel(count, *refs):
    @pl.when(on_late_band())
    def _():
        own_body(count, *refs)


def cross_body(count, target, packed, field, kernel, table, mine, sent, scratch):
    def emit(block, value):
        total = field[:, columns_of(block)] + value
        mine[:, columns_of(block)] = total[:SLAB]
        for k in range(1, MEMBERS):
            sent[k - 1][:, columns_of(block)] = total[k * SLAB : (k + 1) * SLAB].astype(jnp.bfloat16)

    pair_field(
        lax.axis_index("group"), target, packed, minus_occupation(count, packed), lambda: kernel, table, *scratch, emit
    )


def cross_kernel(count, target, packed, field, kernel, table, mine, *rest):
    @pl.when(jnp.logical_not(on_late_band()))
    def _():
        cross_body(count, target, packed, field, kernel, table, mine, rest[: MEMBERS - 1], rest[MEMBERS - 1 :])


def cross_late_kernel(count, target, from_first, from_last, field, kernel, table, held, mine, *rest):
    for packed, here in (
        (from_first, on_last_band()),
        (from_last, jnp.logical_and(on_late_band(), jnp.logical_not(on_last_band()))),
    ):

        @pl.when(here)
        def _():
            cross_body(count, target, packed, field, kernel, table, mine, rest[: MEMBERS - 1], rest[MEMBERS - 1 :])

    @pl.when(jnp.logical_not(on_late_band()))
    def _():
        mine[...] = held[...]


def shape(rows, columns, dtype):
    return jax.ShapeDtypeStruct((rows, columns), dtype)


PAIR_SCRATCH = [pltpu.VMEM((TURNED_ROWS, LANES), jnp.float32), pltpu.VMEM((BLOCKS * N, WIDE), jnp.bfloat16)]
OWN_SCRATCH = [pltpu.VMEM((N, N * N), jnp.int32)] + PAIR_SCRATCH + [pltpu.SemaphoreType.DMA((3,))]
VMEM = pl.BlockSpec(memory_space=pltpu.VMEM)
HBM = pl.BlockSpec(memory_space=pltpu.HBM)


def call(kernel, outs, in_specs, scratch, aliases=None, flops=6 * 2 * N**4):
    return pl.pallas_call(
        kernel,
        out_shape=outs,
        in_specs=in_specs,
        out_specs=[VMEM] * len(outs),
        scratch_shapes=scratch,
        input_output_aliases=aliases or {},
        compiler_params=pltpu.CompilerParams(vmem_limit_bytes=40 * 1024 * 1024),
        cost_estimate=pl.CostEstimate(flops=flops, bytes_accessed=4 * 1024 * 1024, transcendentals=0),
    )


def in_hbm(value):
    return pltpu.with_memory_space_constraint(value, pltpu.HBM)


def sent_along(value, pairs):
    return lax.ppermute(value, ("band", "group"), [(s[0] * MEMBERS + s[1], t[0] * MEMBERS + t[1]) for s, t in pairs])


def next_sources(bands):
    count = lax.axis_size("band")
    return [((b, g), ((b - 1) % count, g ^ 2 if b % ROW == 0 else g)) for b in bands for g in range(MEMBERS)]


def exchanged(sent, bands):
    received = []
    for bits in (2, 3, 1):
        pairs = [((b, g), (b, g ^ bits)) for b in bands for g in range(MEMBERS)]
        received.append(sent_along(sent[bits - 1], pairs))
    return received


def shards(trial, orbitals, labels, kernel_mask):
    bands = lax.axis_size("band")
    count = bands * MEMBERS
    target, table, mask = in_hbm(trial[0]), in_hbm(tables()), in_hbm(kernel_mask)
    source = in_hbm(orbitals[0])

    def packing(late):
        return call(
            functools.partial(pack_kernel, late),
            [shape(N, PACKED, jnp.bfloat16)],
            [pl.BlockSpec(memory_space=pltpu.SMEM), HBM],
            [pltpu.SemaphoreType.DMA((PACK_COPIES,))],
            flops=0,
        )

    packed = packing(False)(labels, source)[0]
    following = sent_along(packed, next_sources(range(1, bands - 1)))
    planes = [
        shape(N, N * N, jnp.float32),
        shape(BLOCKS * N, WIDE, jnp.float32),
        shape(N, N * N, jnp.bfloat16),
        shape(TABLE_ROWS, WIDE, jnp.bfloat16),
    ]
    sources = [HBM, VMEM, HBM, HBM]
    field, kernel, kept_target, kept_table = call(
        functools.partial(own_kernel, count), planes, sources, OWN_SCRATCH
    )(target, packed, mask, table)
    packed, field = lax.optimization_barrier((packed, field))
    from_first = sent_along(packed, next_sources((0,)))
    late_packed = packing(True)(labels, source)[0]
    from_last = sent_along(late_packed, next_sources((bands - 1,)))
    late_field, late_kernel, late_target, late_table = call(
        functools.partial(own_late_kernel, count), planes, sources, OWN_SCRATCH
    )(target, late_packed, mask, table)
    slabs = [shape(SLAB, N * N, jnp.float32)] + [shape(SLAB, N * N, jnp.bfloat16)] * (MEMBERS - 1)
    mine, *sent = call(functools.partial(cross_kernel, count), slabs, [VMEM] * 5, PAIR_SCRATCH)(
        kept_target, following, field, kernel, kept_table
    )
    received = exchanged(sent, range(bands - LATE))
    mine, *sent = call(
        functools.partial(cross_late_kernel, count), slabs, [VMEM] * 7, PAIR_SCRATCH, aliases={6: 0}
    )(late_target, from_first, from_last, late_field, late_kernel, late_table, mine)
    for piece in received + exchanged(sent, range(bands - LATE, bands)):
        mine = mine + piece.astype(jnp.float32)
    return mine[None]


def solution(mesh):
    in_specs = (P("band", None, None), P(("band", "group"), None, None), P(("band", "group")), P())
    out_specs = P("band", "group", None)
    return jax.shard_map(shards, mesh=mesh, in_specs=in_specs, out_specs=out_specs, check_vma=False)
```

```python
import functools

import jax
import jax.numpy as jnp
import numpy as np
from jax import lax
from jax.experimental import pallas as pl
from jax.experimental.pallas import tpu as pltpu
from jax.sharding import PartitionSpec as P


SCREEN_SQUARE = 16.0
N = 64
HALF = 32
LANES = 128
WIDE = 256
BLOCKS = N * N // WIDE
STRIDE = 65
TURNED_ROWS = HALF * STRIDE + N + 8
CHUNK = 256
MEMBERS = 4
SLAB = N // MEMBERS
PACKED = N * N + LANES
PACK_COPIES = 4
LATE = 2
ROW = 8

DIAG, CAS, CAS_ROWS, CAS_COLS, EVEN_FIRST, TABLE_ROWS = 0, 256, 320, 384, 448, 512


def tables():
    k = np.arange(N)
    angle = (k[:, None] * k[None, :] % N).astype(np.float64) * (2.0 * np.pi / N)
    h = (np.cos(angle) + np.sin(angle)) / np.sqrt(float(N))
    order = np.concatenate([np.arange(0, N, 2), np.arange(1, N, 2)])
    table = np.zeros((TABLE_ROWS, WIDE))
    table[DIAG:CAS] = np.kron(np.eye(WIDE // N), h)
    table[CAS:CAS_ROWS, :N] = h
    table[CAS_ROWS:CAS_COLS, :N] = h[order]
    table[CAS_COLS:EVEN_FIRST, :N] = h[:, order]
    table[EVEN_FIRST:, :N] = np.eye(N)[order]
    return jnp.asarray(table, jnp.bfloat16)


def dot(a, b):
    return jnp.dot(a, b, preferred_element_type=jnp.float32)


def low_lanes():
    return lax.broadcasted_iota(jnp.int32, (HALF, LANES), 1) < N


def exchange(top, bottom, low):
    return (
        jnp.where(low, top, pltpu.roll(bottom, N, 1)),
        jnp.where(low, pltpu.roll(top, N, 1), bottom),
    )


def scatter_rows(block, column, turned, low):
    first, second = exchange(block[:HALF], block[HALF:], low)
    turned[pl.ds(2 * column, HALF, stride=STRIDE), :] = first
    turned[pl.ds(2 * column + 1, HALF, stride=STRIDE), :] = second


def gather_rows(column, turned, low):
    first = turned[pl.ds(2 * column, HALF, stride=STRIDE), :].astype(jnp.bfloat16)
    second = turned[pl.ds(2 * column + 1, HALF, stride=STRIDE), :].astype(jnp.bfloat16)
    top, bottom = exchange(first, second, low)
    return jnp.concatenate([top, bottom], axis=0)


def turned_block(block, turned):
    return jnp.concatenate(
        [turned[pl.ds((2 * block + part) * STRIDE, N), :].astype(jnp.bfloat16) for part in range(2)], axis=1
    )


def columns_of(block):
    return slice(block * WIDE, (block + 1) * WIDE)


def by_owner(me, ref, columns):
    return jnp.concatenate([ref[pl.ds((me ^ k) * SLAB, SLAB), columns] for k in range(MEMBERS)], axis=0)


def pair_field(me, target, source, scale, kernel_ready, table, turned, rows, emit):
    low = low_lanes()
    h_diag, h, h_rows = table[DIAG:CAS, :], table[CAS:CAS_ROWS, :N], table[CAS_ROWS:CAS_COLS, :N]
    for block in range(BLOCKS):
        first = dot(h_rows, target[:, columns_of(block)] * source[:, columns_of(block)])
        for part in range(2):
            scatter_rows(first[:, part * LANES : (part + 1) * LANES], 2 * block + part, turned, low)
    for block in range(BLOCKS):
        rows[block * N : (block + 1) * N, :] = dot(h, turned_block(block, turned)).astype(jnp.bfloat16)
    kernel = kernel_ready()
    for chunk in range(BLOCKS * N // CHUNK):
        part = slice(chunk * CHUNK, (chunk + 1) * CHUNK)
        spectrum = dot(rows[part, :], h_diag) * kernel[part, :]
        rows[part, :] = dot(spectrum.astype(jnp.bfloat16), h_diag).astype(jnp.bfloat16)
    for block in range(BLOCKS):
        back = dot(h, rows[block * N : (block + 1) * N, :])
        for part in range(2):
            turned[pl.ds((2 * block + part) * STRIDE, N), :] = back[:, part * LANES : (part + 1) * LANES]
    h_cols = by_owner(me, table.at[CAS_COLS:EVEN_FIRST], slice(0, N))
    for block in range(BLOCKS):
        back = jnp.concatenate(
            [gather_rows(2 * block + part, turned, low) for part in range(2)], axis=1
        )
        potential = dot(h_cols, back)
        emit(block, potential * scale * by_owner(me, source, columns_of(block)).astype(jnp.float32))


def on_last_band():
    return lax.axis_index("band") == lax.axis_size("band") - 1


def on_late_band():
    return lax.axis_index("band") >= lax.axis_size("band") - LATE


def pack_kernel(late, label, source, packed, sems):
    @pl.when(on_late_band() if late else jnp.logical_not(on_last_band()))
    def _():
        step = N * N // PACK_COPIES
        copies = [
            pltpu.make_async_copy(
                source.at[:, i * step : (i + 1) * step], packed.at[:, i * step : (i + 1) * step], sems.at[i]
            )
            for i in range(PACK_COPIES)
        ]
        for copy in copies:
            copy.start()
        for half, part in enumerate((label[0] // 8, label[0] % 8)):
            packed[half * HALF : (half + 1) * HALF, N * N :] = (
                jnp.full((HALF, LANES), part, jnp.int32).astype(jnp.float32).astype(jnp.bfloat16)
            )
        for copy in copies:
            copy.wait()


def minus_occupation(count, packed):
    high, low = (packed[half * HALF : half * HALF + 16, N * N :].astype(jnp.float32) for half in range(2))
    shifted = (8.0 * high + low - count / 2.0) / (count / 4.0)
    return (-1.0 / (1.0 + jnp.exp(shifted)))[:1, :1]


def own_body(count, target, packed, mask, table, field, kernel, target_in, table_in, mask_in, turned, rows, sems):
    copies = [
        pltpu.make_async_copy(a, b, sems.at[i])
        for i, (a, b) in enumerate(((target, target_in), (table, table_in), (mask, mask_in)))
    ]
    for copy in copies:
        copy.start()
    me = lax.axis_index("group")
    low = low_lanes()
    ky = lax.broadcasted_iota(jnp.int32, (N, LANES), 0)
    lane = lax.broadcasted_iota(jnp.int32, (N, LANES), 1)

    def squared(k):
        signed = jnp.where(k < N // 2, k, k - N)
        return signed * signed

    plane = squared(ky) + squared(lane % N)
    for copy in copies:
        copy.wait()
    even_first = table_in[EVEN_FIRST:, :N]
    for block in range(BLOCKS):
        kept = dot(even_first, mask_in[:, columns_of(block)].astype(jnp.float32).astype(jnp.bfloat16))
        for part in range(2):
            scatter_rows(kept[:, part * LANES : (part + 1) * LANES], 2 * block + part, turned, low)
    for half in range(HALF):
        q_square = plane + squared(2 * half + lane // N)
        kept = turned[pl.ds(half * STRIDE, N), :]
        block, part = half // 2, half % 2
        kernel[block * N : (block + 1) * N, part * LANES : (part + 1) * LANES] = (
            kept * SCREEN_SQUARE / (q_square.astype(jnp.float32) + SCREEN_SQUARE)
        )

    def emit(block, value):
        field[:, columns_of(block)] = value

    pair_field(me, target_in, packed, minus_occupation(count, packed), lambda: kernel, table_in, turned, rows, emit)


def own_kernel(count, *refs):
    @pl.when(jnp.logical_not(on_late_band()))
    def _():
        own_body(count, *refs)


def own_late_kernel(count, *refs):
    @pl.when(on_late_band())
    def _():
        own_body(count, *refs)


def cross_body(count, target, packed, field, kernel, table, mine, sent, scratch):
    def emit(block, value):
        total = field[:, columns_of(block)] + value
        mine[:, columns_of(block)] = total[:SLAB]
        for k in range(1, MEMBERS):
            sent[k - 1][:, columns_of(block)] = total[k * SLAB : (k + 1) * SLAB].astype(jnp.bfloat16)

    pair_field(
        lax.axis_index("group"), target, packed, minus_occupation(count, packed), lambda: kernel, table, *scratch, emit
    )


def cross_kernel(count, target, packed, field, kernel, table, mine, *rest):
    @pl.when(jnp.logical_not(on_late_band()))
    def _():
        cross_body(count, target, packed, field, kernel, table, mine, rest[: MEMBERS - 1], rest[MEMBERS - 1 :])


def cross_late_kernel(count, target, from_first, from_last, field, kernel, table, held, mine, *rest):
    for packed, here in (
        (from_first, on_last_band()),
        (from_last, jnp.logical_and(on_late_band(), jnp.logical_not(on_last_band()))),
    ):

        @pl.when(here)
        def _():
            cross_body(count, target, packed, field, kernel, table, mine, rest[: MEMBERS - 1], rest[MEMBERS - 1 :])

    @pl.when(jnp.logical_not(on_late_band()))
    def _():
        mine[...] = held[...]


def shape(rows, columns, dtype):
    return jax.ShapeDtypeStruct((rows, columns), dtype)


PAIR_SCRATCH = [pltpu.VMEM((TURNED_ROWS, LANES), jnp.float32), pltpu.VMEM((BLOCKS * N, WIDE), jnp.bfloat16)]
OWN_SCRATCH = [pltpu.VMEM((N, N * N), jnp.int32)] + PAIR_SCRATCH + [pltpu.SemaphoreType.DMA((3,))]
VMEM = pl.BlockSpec(memory_space=pltpu.VMEM)
HBM = pl.BlockSpec(memory_space=pltpu.HBM)


def call(kernel, outs, in_specs, scratch, aliases=None, flops=6 * 2 * N**4):
    return pl.pallas_call(
        kernel,
        out_shape=outs,
        in_specs=in_specs,
        out_specs=[VMEM] * len(outs),
        scratch_shapes=scratch,
        input_output_aliases=aliases or {},
        compiler_params=pltpu.CompilerParams(vmem_limit_bytes=40 * 1024 * 1024),
        cost_estimate=pl.CostEstimate(flops=flops, bytes_accessed=4 * 1024 * 1024, transcendentals=0),
    )


def in_hbm(value):
    return pltpu.with_memory_space_constraint(value, pltpu.HBM)


def sent_along(value, pairs):
    return lax.ppermute(value, ("band", "group"), [(s[0] * MEMBERS + s[1], t[0] * MEMBERS + t[1]) for s, t in pairs])


def next_sources(bands):
    count = lax.axis_size("band")
    return [((b, g), ((b - 1) % count, g ^ 2 if b % ROW == 0 else g)) for b in bands for g in range(MEMBERS)]


def exchanged(sent, bands):
    received = []
    for bits in (3, 2, 1):
        pairs = [((b, g), (b, g ^ bits)) for b in bands for g in range(MEMBERS)]
        received.append(sent_along(sent[bits - 1], pairs))
    return received


def shards(trial, orbitals, labels, kernel_mask):
    bands = lax.axis_size("band")
    count = bands * MEMBERS
    target, table, mask = in_hbm(trial[0]), in_hbm(tables()), in_hbm(kernel_mask)
    source = in_hbm(orbitals[0])

    def packing(late):
        return call(
            functools.partial(pack_kernel, late),
            [shape(N, PACKED, jnp.bfloat16)],
            [pl.BlockSpec(memory_space=pltpu.SMEM), HBM],
            [pltpu.SemaphoreType.DMA((PACK_COPIES,))],
            flops=0,
        )

    packed = packing(False)(labels, source)[0]
    following = sent_along(packed, next_sources(range(1, bands - 1)))
    planes = [
        shape(N, N * N, jnp.float32),
        shape(BLOCKS * N, WIDE, jnp.float32),
        shape(N, N * N, jnp.bfloat16),
        shape(TABLE_ROWS, WIDE, jnp.bfloat16),
    ]
    sources = [HBM, VMEM, HBM, HBM]
    field, kernel, kept_target, kept_table = call(
        functools.partial(own_kernel, count), planes, sources, OWN_SCRATCH
    )(target, packed, mask, table)
    packed, field = lax.optimization_barrier((packed, field))
    from_first = sent_along(packed, next_sources((0,)))
    late_packed = packing(True)(labels, source)[0]
    from_last = sent_along(late_packed, next_sources((bands - 1,)))
    late_field, late_kernel, late_target, late_table = call(
        functools.partial(own_late_kernel, count), planes, sources, OWN_SCRATCH
    )(target, late_packed, mask, table)
    slabs = [shape(SLAB, N * N, jnp.float32)] + [shape(SLAB, N * N, jnp.bfloat16)] * (MEMBERS - 1)
    mine, *sent = call(functools.partial(cross_kernel, count), slabs, [VMEM] * 5, PAIR_SCRATCH)(
        kept_target, following, field, kernel, kept_table
    )
    received = exchanged(sent, range(bands - LATE))
    mine, *sent = call(
        functools.partial(cross_late_kernel, count), slabs, [VMEM] * 7, PAIR_SCRATCH, aliases={6: 0}
    )(late_target, from_first, from_last, late_field, late_kernel, late_table, mine)
    for piece in received + exchanged(sent, range(bands - LATE, bands)):
        mine = mine + piece.astype(jnp.float32)
    return mine[None]


def solution(mesh):
    in_specs = (P("band", None, None), P(("band", "group"), None, None), P(("band", "group")), P())
    out_specs = P("band", "group", None)
    return jax.shard_map(shards, mesh=mesh, in_specs=in_specs, out_specs=out_specs, check_vma=False)
```
